256 devices in a mesh: seq: 32 (over z, x), head: 8 (over y, core).
Axes of the slice: x: 4, y: 4, z: 8, core: 2. Of those that a mesh axis runs over, the one named last changes fastest.
Arguments:
- query: bfloat16 [8, 16384, 128], P('head', 'seq'), may hold values from -8 to 8
- key: bfloat16 [8, 16384, 128], P('head', 'seq'), may hold values from -8 to 8
- value: bfloat16 [8, 16384, 128], P('head', 'seq'), may hold values from -16 to 16
- lin_query: bfloat16 [8, 16384, 128], P('head', 'seq'), may hold values from -52 to 52
- lin_key: bfloat16 [8, 16384, 128], P('head', 'seq'), may hold values from -5 to 5
- gain: float32 [8, 128], P('head'), may hold values from 0.25 to 1.75
- cotangent: bfloat16 [8, 16384, 128], P('head', 'seq'), may hold values from -16 to 16
- key_block: int32 [128, 20], replicated, may hold values from -1 to 127, as said below
Outputs:
- mixed: bfloat16 [8, 16384, 128], P('head', 'seq')
- grad_query: bfloat16 [8, 16384, 128], P('head', 'seq')
- grad_key: bfloat16 [8, 16384, 128], P('head', 'seq')
- grad_value: bfloat16 [8, 16384, 128], P('head', 'seq')
- grad_lin_query: bfloat16 [8, 16384, 128], P('head', 'seq')
- grad_lin_key: bfloat16 [8, 16384, 128], P('head', 'seq')
- grad_gain: float32 [8, 128], P('head')
The draws below stay inside these ranges and needn't reach their ends.
Inputs may be any that keep to these rules, and one draw needn't show every extreme that they name: `key_block`: row b lists the key blocks that query block b reads: slot 0 is b, slot 1 is b - 1 (-1 when b is 0); each later slot names a block that lies on an earlier index of seq than b and before b - 1, or is -1, and all -1 slots follow the named ones. A row names no block twice. Over all rows' slots from 2 on, at most one block of the blocks on one index of seq is named.
All inputs are finite; a program needn't handle non-finite values.
Results may differ from the reference program's by a relative error of at most 0.039.
Values may be sent and summed in bfloat16 or wider, within the bound.
No kernel may reach another device: no remote copies, remote signals or barrier semaphores. Data moves between devices by JAX's collectives and lax.ppermute only.
A program may use at most 64 MiB of HBM per device.

```python
import math
import jax
import jax.numpy as jnp
from jax import lax

HEAD_DIM = 128
TOK_DEV = 512
BLK = 128
SEL = 20
HEADS = 8
TOKENS = 16384
NBLK = 128


def score_pair(key):
    base = jax.random.fold_in(key, 11)
    key_q, key_k = jax.random.split(base, 2)
    shape = (HEADS, TOKENS, HEAD_DIM)
    queries = jnp.clip(jax.random.normal(key_q, shape, jnp.float32), -6.0, 6.0)
    keys = jnp.clip(jax.random.normal(key_k, shape, jnp.float32), -6.0, 6.0)
    return (queries, keys)


def draw_query(key, part):
    return score_pair(key)[0].astype(jnp.bfloat16)


def draw_key(key, part):
    return score_pair(key)[1].astype(jnp.bfloat16)


def draw_value(key, part):
    key_v, key_c = jax.random.split(jax.random.fold_in(key, 23))
    shape = (HEADS, TOKENS, HEAD_DIM)
    column = jnp.exp(jax.random.uniform(key_c, (HEADS, 1, HEAD_DIM), jnp.float32, 0.0, math.log(10.0))) / 3.0
    basic = jnp.clip(jax.random.normal(key_v, shape, jnp.float32), -4.0, 4.0)
    return jnp.clip(basic * column, -16.0, 16.0).astype(jnp.bfloat16)


def draw_lin_query(key, part):
    key_v, key_r = jax.random.split(jax.random.fold_in(key, 31))
    shape = (HEADS, TOKENS, HEAD_DIM)
    row = jnp.exp(jax.random.uniform(key_r, (HEADS, TOKENS, 1), jnp.float32, 0.0, math.log(10.0))) / 3.0
    factor = 1.0 + 2.0 * jnp.arange(HEADS).astype(jnp.float32) / max(HEADS - 1, 1)
    basic = jnp.clip(jax.random.normal(key_v, shape, jnp.float32), -4.0, 4.0)
    return jnp.clip(basic * row * factor[:, None, None], -52.0, 52.0).astype(jnp.bfloat16)


def draw_cotangent(key, part):
    key_v = jax.random.fold_in(key, 41)
    shape = (HEADS, TOKENS, HEAD_DIM)
    ramp = 1.0 + 2.0 * jnp.arange(TOKENS).astype(jnp.float32) / TOKENS
    basic = jnp.clip(jax.random.normal(key_v, shape, jnp.float32), -4.0, 4.0)
    return jnp.clip(basic * ramp[None, :, None], -16.0, 16.0).astype(jnp.bfloat16)


def draw_key_block(key, part):
    per_dev = TOK_DEV // BLK
    owners = NBLK // per_dev
    key_c, key_s = jax.random.split(jax.random.fold_in(key, 5))
    chosen = jax.random.randint(key_c, (owners,), 0, per_dev) + jnp.arange(owners) * per_dev
    rows = jnp.arange(NBLK)
    owner = rows // per_dev
    places = jnp.arange(owners)
    valid = (places[None, :] < owner[:, None]) & (chosen[None, :] < rows[:, None] - 1)
    score = jax.random.randint(key_s, (NBLK, owners), 0, 1 << 20) * owners + places[None, :]
    score = jnp.where(valid, score, -1 - places[None, :])
    picks = min(SEL - 2, owners)
    top_score, top_place = lax.top_k(score, picks)
    far = jnp.where(top_score >= 0, chosen[top_place], -1)
    if SEL - 2 > picks:
        far = jnp.concatenate([far, jnp.full((NBLK, SEL - 2 - picks), -1, far.dtype)], axis=1)
    local = jnp.stack([rows, rows - 1], axis=1)
    return jnp.concatenate([local, far], axis=1).astype(jnp.int32)


def shard_levels(rng, extent, pieces, smallest, top_value):
    factor_of, own = 1.0, jax.random.fold_in(rng, 6)
    for dim, shards_of in pieces:
        heights = jnp.exp(jax.random.uniform(jax.random.fold_in(own, dim), (shards_of,), jnp.float32, smallest / len(pieces), top_value / len(pieces)))
        factor_of = factor_of * jnp.repeat(heights, extent[dim] // shards_of).reshape([-1 if axis == dim else 1 for axis in range(len(extent))])
    return factor_of


def gaussian(own_key, dims, deviation, reach, shards=(), kind=jnp.bfloat16):
    array = jax.random.normal(own_key, dims, jnp.float32) * deviation
    if len(shards) > 0:
        array = shard_levels(own_key, dims, shards, -0.22, 0.18) * array
    return jnp.clip(array, min=-reach, max=reach).astype(kind)


def setup_inputs(seed: int = 0) -> dict:
    key_list = jax.random.split(jax.random.key(seed), 9)
    return {
        "query": draw_query(jax.random.fold_in(key_list[8], 71), 0),
        "key": draw_key(jax.random.fold_in(key_list[8], 71), 0),
        "value": draw_value(jax.random.fold_in(key_list[8], 71), 0),
        "lin_query": draw_lin_query(jax.random.fold_in(key_list[8], 71), 0),
        "lin_key": gaussian(key_list[4], (HEADS, TOKENS, HEAD_DIM), 1.0, 5.0, ((0, 8), (1, 32))),
        "gain": jnp.clip(1.0 + 0.15 * jax.random.normal(key_list[5], (HEADS, HEAD_DIM), jnp.float32), 0.25, 1.75),
        "cotangent": draw_cotangent(jax.random.fold_in(key_list[8], 71), 0),
        "key_block": draw_key_block(jax.random.fold_in(key_list[8], 71), 0),
    }


masked_value = -1e+30
eps_norm = 1e-05

def allowed_rows(names):
    live = names >= 0
    causal = jnp.arange(BLK)[:, None] >= jnp.arange(BLK)[None, :]
    first = jnp.arange(SEL) == 0
    return live[None, :, None] & (jnp.logical_not(first)[None, :, None] | causal[:, None, :])

def reference(query, key, value, lin_query, lin_key, gain, cotangent, key_block):
    f32 = jnp.float32
    bf16 = jnp.bfloat16
    hi = lax.Precision.HIGHEST
    heads = query.shape[0]
    scale = HEAD_DIM ** (-0.5)
    features = heads * HEAD_DIM

    def blocks(x):
        return x.reshape(heads, NBLK, BLK, HEAD_DIM).transpose(1, 0, 2, 3)

    def unblocks(x):
        return x.transpose(1, 0, 2, 3).reshape(heads, TOKENS, HEAD_DIM)
    query_b = blocks(query)
    key_b = blocks(key)
    value_b = blocks(value)
    order = jnp.arange(NBLK, dtype=jnp.int32)

    def scores_of(b):
        names = key_block[b]
        index = jnp.maximum(names, 0).astype(jnp.int32)
        rows_q = query_b[b].astype(f32)
        keys_g = key_b[index].astype(f32)
        values_g = value_b[index].astype(f32)
        scores = jnp.einsum('hqd,jhkd->hqjk', rows_q, keys_g, precision=hi) * scale
        scores = jnp.where(allowed_rows(names)[None], scores, masked_value)
        return (index, rows_q, keys_g, values_g, scores)

    def attend(b):
        index, rows_q, keys_g, values_g, scores = scores_of(b)
        row_max = lax.optimization_barrier(jnp.max(scores, axis=(2, 3), keepdims=True))
        weights = jnp.exp(scores - row_max)
        total = lax.optimization_barrier(jnp.sum(weights, axis=(2, 3), keepdims=True))
        weights_b = lax.optimization_barrier(weights.astype(bf16)).astype(f32)
        summed = jnp.einsum('hqjk,jhkd->hqd', weights_b, values_g, precision=hi)
        attended = (summed / total[..., 0]).astype(bf16)
        log_total = (row_max + jnp.log(total))[..., 0, 0]
        return (attended, log_total)
    attended, log_total = lax.map(attend, order)
    att_f = attended.astype(f32)
    lq_all = blocks(lin_query).astype(f32)
    lk_all = blocks(lin_key).astype(f32)
    lower = (jnp.arange(BLK)[:, None] >= jnp.arange(BLK)[None, :]).astype(f32)
    zero_state = jnp.zeros((heads, HEAD_DIM, HEAD_DIM), f32)

    def run(state, piece):
        lq, lk, vo = piece
        mixing = jnp.einsum('hqi,hki->hqk', lq, lk, precision=hi) * lower
        out = jnp.einsum('hqk,hkd->hqd', mixing, vo, precision=hi) + jnp.einsum('hqi,hij->hqj', lq, state, precision=hi)
        return (state + jnp.einsum('hki,hkj->hij', lk, vo, precision=hi), (out, state))
    final_state, (linear, prior) = lax.scan(run, zero_state, (lq_all, lk_all, att_f))
    squares = lax.optimization_barrier(jnp.sum(linear * linear, axis=(1, 3)))
    inv_rms = lax.rsqrt(squares / features + eps_norm)
    normed = linear * inv_rms[:, None, :, None]
    mixed = (att_f + gain[None, :, None, :] * normed).astype(bf16)
    grad_out = blocks(cotangent).astype(f32)
    grad_gain = lax.optimization_barrier(jnp.sum(grad_out * normed, axis=(0, 2)))
    scaled = grad_out * gain[None, :, None, :]
    inner = lax.optimization_barrier(jnp.sum(scaled * normed, axis=(1, 3)))
    grad_linear = inv_rms[:, None, :, None] * (scaled - normed * (inner / features)[:, None, :, None])

    def back(after, piece):
        lq, lk, vo, glin, before = piece
        mixing = jnp.einsum('hqi,hki->hqk', lq, lk, precision=hi) * lower
        pairs = jnp.einsum('hqd,hkd->hqk', glin, vo, precision=hi) * lower
        g_lq = jnp.einsum('hqk,hki->hqi', pairs, lk, precision=hi) + jnp.einsum('hqj,hij->hqi', glin, before, precision=hi)
        g_lk = jnp.einsum('hqk,hqi->hki', pairs, lq, precision=hi) + jnp.einsum('hkj,hij->hki', vo, after, precision=hi)
        g_att = jnp.einsum('hqk,hqd->hkd', mixing, glin, precision=hi) + jnp.einsum('hki,hij->hkj', lk, after, precision=hi)
        return (after + jnp.einsum('hti,htj->hij', lq, glin, precision=hi), (g_lq, g_lk, g_att))
    first_state, (g_lq, g_lk, g_att) = lax.scan(back, zero_state, (lq_all, lk_all, att_f, grad_linear, prior), reverse=True)
    grad_att = (grad_out + g_att).astype(bf16)
    grad_att_f = grad_att.astype(f32)
    delta = lax.optimization_barrier(jnp.sum(grad_att_f * att_f, axis=3))

    def grads(carry, b):
        acc_key, acc_value = carry
        index, rows_q, keys_g, values_g, scores = scores_of(b)
        probs = jnp.exp(scores - log_total[b][..., None, None])
        probs_b = lax.optimization_barrier(probs.astype(bf16)).astype(f32)
        go = grad_att_f[b]
        grad_probs = jnp.einsum('hqd,jhkd->hqjk', go, values_g, precision=hi)
        grad_scores = probs * (grad_probs - delta[b][..., None, None])
        grad_scores = lax.optimization_barrier(grad_scores.astype(bf16)).astype(f32)
        gq = (jnp.einsum('hqjk,jhkd->hqd', grad_scores, keys_g, precision=hi) * scale).astype(bf16)
        gk = jnp.einsum('hqjk,hqd->jhkd', grad_scores, rows_q, precision=hi) * scale
        gv = jnp.einsum('hqjk,hqd->jhkd', probs_b, go, precision=hi)
        return ((acc_key.at[index].add(gk), acc_value.at[index].add(gv)), gq)
    zero_grads = jnp.zeros((NBLK, heads, BLK, HEAD_DIM), f32)
    (acc_key, acc_value), grad_q = lax.scan(grads, (zero_grads, zero_grads), order)
    return (unblocks(mixed), unblocks(grad_q), unblocks(acc_key.astype(bf16)), unblocks(acc_value.astype(bf16)), unblocks(g_lq.astype(bf16)), unblocks(g_lk.astype(bf16)), grad_gain)
```

```python
import functools

import jax
import jax.numpy as jnp
from jax import lax
from jax.experimental import pallas as pl
from jax.experimental.pallas import tpu as pltpu
from jax.sharding import Mesh, PartitionSpec as P

BLK = 128
NZ, NX, NY, NC = 8, 4, 4, 2
masked_value = -1e30
eps_norm = 1e-05
f32 = jnp.float32
bf16 = jnp.bfloat16
NT = (((1,), (1,)), ((), ()))
TN = (((0,), (0,)), ((), ()))
VM = pl.BlockSpec(memory_space=pltpu.VMEM)
SM = pl.BlockSpec(memory_space=pltpu.SMEM)
AN = pl.BlockSpec(memory_space=pl.ANY)
FAR = NZ * NX
OWN = FAR
PREV = FAR + 4
POOL = FAR + 5


def mm(a, b, dims=None):
    if dims is None:
        return jnp.dot(a, b, preferred_element_type=f32)
    return lax.dot_general(a, b, dims, preferred_element_type=f32)


def call(body, outs, ins, specs, scratch=()):
    return pl.pallas_call(
        body,
        out_shape=[jax.ShapeDtypeStruct(s, d) for s, d in outs],
        in_specs=list(specs),
        out_specs=[VM] * len(outs),
        scratch_shapes=list(scratch),
        compiler_params=pltpu.CompilerParams(vmem_limit_bytes=40 << 20),
    )(*ins)


def rows(b):
    return pl.ds(b * BLK, BLK)


def as_row(col):
    return jnp.broadcast_to(col, (BLK, BLK)).T[0:1]


def as_cols(row):
    return jnp.broadcast_to(row, (BLK, BLK)).T


def lower_mask():
    return lax.broadcasted_iota(jnp.int32, (BLK, BLK), 0) >= lax.broadcasted_iota(
        jnp.int32, (BLK, BLK), 1
    )


def pick_kernel(pos, names, k, v, lk, lq, kv, lkt, lqt):
    base = pos[0] * 16 + pos[1] * 4
    far = names[...]
    col = lax.broadcasted_iota(jnp.int32, far.shape, 1)
    hit = (col >= 2) & (far >= base) & (far < base + 4)
    mine = jnp.max(jnp.where(hit, far - base, 0).astype(f32)).astype(jnp.int32)
    kv[0:BLK] = k[rows(mine), :]
    kv[BLK:] = v[rows(mine), :]
    lkt[...] = lk[...].T
    lqt[...] = lq[...].T


def place_of(pos, names, b, j):
    name = names[b, j]
    base = pos[0] * 16 + pos[1] * 4
    live = name >= 0
    if j == 0:
        return OWN + b, live
    if j == 1:
        place = jnp.where(name >= base, OWN + name - base, PREV)
        return jnp.where(live, place, OWN), live
    back_z = jnp.bitwise_and(pos[0] - jnp.right_shift(name, 4), NZ - 1)
    back_x = jnp.bitwise_and(pos[1] - jnp.bitwise_and(jnp.right_shift(name, 2), 3), NX - 1)
    return jnp.where(live, back_x * NZ + back_z, OWN), live


def pool_copies(far, k, v, prev, pool, sems):
    copies = [
        pltpu.make_async_copy(f, pool.at[pl.ds(NZ * j, NZ)], sems.at[j])
        for j, f in enumerate(far)
    ]
    copies.append(pltpu.make_async_copy(k, pool.at[pl.ds(OWN, 4), pl.ds(0, BLK)], sems.at[NX]))
    copies.append(
        pltpu.make_async_copy(v, pool.at[pl.ds(OWN, 4), pl.ds(BLK, BLK)], sems.at[NX + 1])
    )
    copies.append(pltpu.make_async_copy(prev, pool.at[PREV], sems.at[NX + 2]))
    for c in copies:
        c.start()
    for c in copies:
        c.wait()


GROUP = 4


def attend_kernel(pos, names, q, lkt, f0, f1, f2, f3, k, v, prev, att, lse, state, pool, s_scr, sems):
    pool_copies((f0, f1, f2, f3), k, v, prev, pool, sems)
    nsel = names.shape[1]
    scale = BLK ** (-0.5)

    def block(b, carry):
        qb = q[rows(b), :]
        top = None
        for g in range(0, nsel, GROUP):
            spots = [place_of(pos, names, b, j) for j in range(g, g + GROUP)]
            keys = jnp.concatenate([pool[p, 0:BLK, :] for p, _ in spots], axis=0)
            s = mm(qb, keys, NT)
            for i, (_, live) in enumerate(spots):
                j = g + i
                piece = s[:, i * BLK : (i + 1) * BLK] * scale + jnp.where(live, 0.0, masked_value)
                if j == 0:
                    piece = jnp.where(lower_mask(), piece, masked_value)
                s_scr[:, j * BLK : (j + 1) * BLK] = piece
                top = piece if top is None else jnp.maximum(top, piece)
        row_max = jnp.max(top, axis=1, keepdims=True)
        part = jnp.zeros((BLK, BLK), f32)
        acc = jnp.zeros((BLK, BLK), f32)
        for g in range(0, nsel, GROUP):
            w = jnp.exp(s_scr[:, g * BLK : (g + GROUP) * BLK] - row_max)
            for i in range(GROUP):
                part = part + w[:, i * BLK : (i + 1) * BLK]
            vals = jnp.concatenate(
                [pool[place_of(pos, names, b, j)[0], BLK:, :] for j in range(g, g + GROUP)], axis=0
            )
            acc = acc + mm(w.astype(bf16), vals)
        total = jnp.sum(part, axis=1, keepdims=True)
        att[rows(b), :] = (acc / total).astype(bf16)
        lse[pl.ds(b, 1), :] = as_row(row_max + jnp.log(total))
        return carry

    lax.fori_loop(0, 4, block, 0)
    state[...] = mm(lkt[...], att[...])


def linear_kernel(pos, lq, lk, lkt, att, gain, cot, x0, x1, x2, x3, z1, z2, z3, z4, z5, z6, z7,
                  lin, prior, mix, sums):
    lower = lower_mask()
    run = jnp.zeros((BLK, BLK), f32)
    for j, r in enumerate((x1, x2, x3)):
        run = run + jnp.where(pos[1] > j, r[...], 0.0)
    for j, r in enumerate((z1, z2, z3, z4, z5, z6, z7)):
        run = run + jnp.where(pos[0] > j, r[...].astype(f32), 0.0)
    sums[...] = jnp.zeros((8, BLK), f32)
    for b in range(4):
        r = slice(b * BLK, (b + 1) * BLK)
        before = run.astype(bf16)
        prior[b] = before
        mixing = jnp.where(lower, mm(lq[r], lk[r], NT), 0.0).astype(bf16)
        mix[b] = mixing
        out = mm(mixing, att[r]) + mm(lq[r], before)
        lin[r] = out
        if b < 3:
            run = run + mm(lkt[:, r], att[r])
        scaled = cot[r].astype(f32) * gain[...]
        sums[b : b + 1] = as_row(jnp.sum(out * out, axis=1, keepdims=True))
        sums[4 + b : 5 + b] = as_row(jnp.sum(out * scaled, axis=1, keepdims=True))


def norm_terms(sums, features):
    inv = lax.rsqrt(sums[0:4] / features + eps_norm)
    return inv, inv * inv * inv * sums[4:8] / features


def norm_kernel(features, lqt, lin, gain, cot, s0, s1, s2, s3, glin, inv_out, send, local):
    inv, pull = norm_terms(s0[...] + s1[...] + s2[...] + s3[...], features)
    inv_out[0:4] = inv
    inv_out[4:8] = inv
    ggain = jnp.zeros((1, BLK), f32)
    for b in range(4):
        r = slice(b * BLK, (b + 1) * BLK)
        c = cot[r].astype(f32)
        out = lin[r]
        invc = as_cols(inv[b : b + 1])
        ggain = ggain + jnp.sum(c * (out * invc), axis=0, keepdims=True)
        glin[r] = (invc * (c * gain[...]) - out * as_cols(pull[b : b + 1])).astype(bf16)
    run = jnp.zeros((BLK, BLK), f32)
    for b in range(3, -1, -1):
        r = slice(b * BLK, (b + 1) * BLK)
        local[b] = run
        run = run + mm(lqt[:, r], glin[r])
    send[0:BLK] = run
    send[BLK:] = jnp.broadcast_to(ggain, (8, BLK))


def side_kernel(inv, lin, gain, att, glin, lk, lq, prior, mixed, dlq, pairs_t, mix_t):
    lower = lower_mask()
    upper = lax.broadcasted_iota(jnp.int32, (BLK, BLK), 0) <= lax.broadcasted_iota(
        jnp.int32, (BLK, BLK), 1
    )
    for b in range(4):
        r = slice(b * BLK, (b + 1) * BLK)
        normed = lin[r] * as_cols(inv[b : b + 1])
        mixed[r] = (att[r].astype(f32) + gain[...] * normed).astype(bf16)
        pairs = jnp.where(lower, mm(glin[r], att[r], NT), 0.0).astype(bf16)
        dlq[r] = (mm(pairs, lk[r]) + mm(glin[r], prior[b], NT)).astype(bf16)
        pairs_t[b] = jnp.where(upper, mm(att[r], glin[r], NT), 0.0).astype(bf16)
        mix_t[b] = jnp.where(upper, mm(lk[r], lq[r], NT), 0.0).astype(bf16)


def backward_kernel(pos, names, q, lse, att, cot, lq, lk, glin, pairs_t, mix_t, local,
                    x0, x1, x2, x3, z0, z1, z2, z3, z4, z5, z6, z7,
                    f0, f1, f2, f3, k, v, prev,
                    dlk, dq, o0, o1, o2, o3, own, back, ggain, pool, acc, gatt, delta, sems):
    copies_done = pool_copies((f0, f1, f2, f3), k, v, prev, pool, sems)
    nsel = names.shape[1]
    scale = BLK ** (-0.5)
    later = jnp.zeros((BLK, BLK), f32)
    for j, r in enumerate((x1, x2, x3)):
        later = later + jnp.where(pos[1] + j + 1 < NX, r[0:BLK], 0.0)
    gg = z0[BLK : BLK + 8].astype(f32)
    for j, r in enumerate((z1, z2, z3, z4, z5, z6, z7)):
        later = later + jnp.where(pos[0] + j + 1 < NZ, r[0:BLK].astype(f32), 0.0)
        gg = gg + r[BLK : BLK + 8].astype(f32)
    ggain[...] = gg
    for b in range(4):
        r = slice(b * BLK, (b + 1) * BLK)
        after = (later + local[b]).astype(bf16)
        dlk[r] = (mm(pairs_t[b], lq[r]) + mm(att[r], after, NT)).astype(bf16)
        g = cot[r].astype(f32) + mm(mix_t[b], glin[r]) + mm(lk[r], after)
        g = g.astype(bf16)
        gatt[r] = g
        delta[b : b + 1] = as_row(
            jnp.sum(g.astype(f32) * att[r].astype(f32), axis=1, keepdims=True)
        )
    acc[...] = jnp.zeros(acc.shape, f32)

    def block(b, carry):
        qb = q[rows(b), :]
        gb = gatt[rows(b), :]
        lse_b = lse[pl.ds(b, 1), :]
        delta_b = delta[pl.ds(b, 1), :]
        dqb = jnp.zeros((BLK, BLK), f32)
        for g in range(0, nsel, GROUP):
            spots = [place_of(pos, names, b, j) for j in range(g, g + GROUP)]
            keys = jnp.concatenate([pool[p, 0:BLK, :] for p, _ in spots], axis=0)
            vals = jnp.concatenate([pool[p, BLK:, :] for p, _ in spots], axis=0)
            s = mm(keys, qb, NT)
            dp = mm(vals, gb, NT)
            pieces = []
            for i, (_, live) in enumerate(spots):
                r = slice(i * BLK, (i + 1) * BLK)
                piece = s[r] * scale + jnp.where(live, 0.0, masked_value)
                if g + i == 0:
                    keep = lax.broadcasted_iota(jnp.int32, (BLK, BLK), 0) <= lax.broadcasted_iota(
                        jnp.int32, (BLK, BLK), 1
                    )
                    piece = jnp.where(keep, piece, masked_value)
                pieces.append(jnp.exp(piece - lse_b))
            p = jnp.concatenate(pieces, axis=0)
            ds = (p * (dp - delta_b)).astype(bf16)
            dv = mm(p.astype(bf16), gb)
            dk = mm(ds, qb)
            dqb = dqb + mm(ds, keys, TN)
            for i, (spot, _) in enumerate(spots):
                r = slice(i * BLK, (i + 1) * BLK)
                acc[spot, 0:BLK, :] += dk[r]
                acc[spot, BLK:, :] += dv[r]
        dq[rows(b), :] = (dqb * scale).astype(bf16)
        return carry

    lax.fori_loop(0, 4, block, 0)
    for j, o in enumerate((o0, o1, o2, o3)):
        o[:, 0:BLK, :] = (acc[NZ * j : NZ * (j + 1), 0:BLK, :] * scale).astype(bf16)
        o[:, BLK:, :] = acc[NZ * j : NZ * (j + 1), BLK:, :].astype(bf16)
    own[:, 0:BLK, :] = acc[OWN : OWN + 4, 0:BLK, :] * scale
    own[:, BLK:, :] = acc[OWN : OWN + 4, BLK:, :]
    back[0:BLK] = (acc[PREV, 0:BLK, :] * scale).astype(bf16)
    back[BLK:] = acc[PREV, BLK:, :].astype(bf16)


def fold_kernel(a0, a1, a2, a3, *outs):
    for i, o in enumerate(outs):
        o[...] = (
            a0[i].astype(f32) + a1[i].astype(f32) + a2[i].astype(f32) + a3[i].astype(f32)
        ).astype(bf16)


def finish_kernel(pos, names, own, back, e0, e1, e2, e3, e4, e5, e6, e7, gk, gv):
    base = pos[0] * 16 + pos[1] * 4
    far = names[...]
    col = lax.broadcasted_iota(jnp.int32, far.shape, 1)
    hit = (col >= 2) & (far >= base) & (far < base + 4)
    mine = jnp.max(jnp.where(hit, far - base, 0).astype(f32)).astype(jnp.int32)
    gathered = e0[...].astype(f32)
    for e in (e1, e2, e3, e4, e5, e6, e7):
        gathered = gathered + e[...].astype(f32)
    for b in range(4):
        total = own[b] + jnp.where(mine == b, gathered, 0.0)
        if b == 3:
            total = total + back[...].astype(f32)
        gk[b * BLK : (b + 1) * BLK] = total[0:BLK].astype(bf16)
        gv[b * BLK : (b + 1) * BLK] = total[BLK:].astype(bf16)


def turn(value, axis, size, by):
    return lax.ppermute(value, axis, [(i, (i + by) % size) for i in range(size)])


def per_device(query, key, value, lin_query, lin_key, gain, cotangent, key_block):
    q, k, v, lq, lk, cot = (a[0] for a in (query, key, value, lin_query, lin_key, cotangent))
    width = q.shape[1]
    seq = ("z", "x")
    zi = lax.axis_index("z")
    xi = lax.axis_index("x")
    pos = jnp.stack([zi, xi]).astype(jnp.int32)
    features = float(NY * NC * width)
    names = lax.dynamic_slice_in_dim(key_block, (zi * NX + xi) * 4, 4, 0)
    k4 = k.reshape(4, BLK, width)
    v4 = v.reshape(4, BLK, width)
    tile = (BLK, BLK)

    kv, lkt, lqt = call(
        pick_kernel,
        [((2 * BLK, width), bf16), ((width, 512), bf16), ((width, 512), bf16)],
        (pos, key_block, k, v, lk, lq),
        [SM, VM, VM, VM, VM, VM],
    )
    last = jnp.concatenate([k4[3], v4[3]], axis=0)
    prev = lax.ppermute(last, seq, [(i, i + 1) for i in range(NZ * NX - 1)])
    col = jnp.stack([kv] + [turn(kv, "z", NZ, i) for i in range(1, NZ)])
    far = [col] + [turn(col, "x", NX, j) for j in range(1, NX)]

    pool_scratch = [pltpu.VMEM((POOL, 2 * BLK, width), bf16)]
    sems = [pltpu.SemaphoreType.DMA((NX + 3,))]
    att, lse, state = call(
        attend_kernel,
        [((512, width), bf16), ((8, BLK), f32), (tile, f32)],
        (pos, names, q, lkt, *far, k4, v4, prev),
        [SM, SM, VM, VM] + [AN] * 7,
        pool_scratch + [pltpu.VMEM((BLK, names.shape[1] * BLK), f32)] + sems,
    )

    xs = [state] + [turn(state, "x", NX, j) for j in range(1, NX)]
    row_state = (xs[0] + xs[1] + xs[2] + xs[3]).astype(bf16)
    zs = [turn(row_state, "z", NZ, i) for i in range(1, NZ)]
    lin, prior, mix, sums = call(
        linear_kernel,
        [((512, width), f32), ((4, BLK, width), bf16), ((4, BLK, BLK), bf16), ((8, BLK), f32)],
        (pos, lq, lk, lkt, att, gain, cot, *xs, *zs),
        [SM] + [VM] * 17,
    )
    sums = sums + turn(sums, "c", NC, 1)
    ys = [sums] + [turn(sums, "y", NY, i) for i in range(1, NY)]
    glin, inv, send, local = call(
        functools.partial(norm_kernel, features),
        [((512, width), bf16), ((8, BLK), f32), ((BLK + 8, BLK), f32), ((4, BLK, BLK), f32)],
        (lqt, lin, gain, cot, *ys),
        [VM] * 8,
    )
    ex = [send] + [turn(send, "x", NX, -j) for j in range(1, NX)]
    row_send = ex[0] + ex[1] + ex[2] + ex[3]
    ez = [row_send] + [turn(row_send, "z", NZ, -i) for i in range(1, NZ)]
    mixed, dlq, pairs_t, mix_t = call(
        side_kernel,
        [((512, width), bf16), ((512, width), bf16), ((4, BLK, BLK), bf16), ((4, BLK, BLK), bf16)],
        (inv, lin, gain, att, glin, lk, lq, prior),
        [VM] * 8,
    )
    outs = call(
        backward_kernel,
        [((512, width), bf16), ((512, width), bf16)]
        + [((NZ, 2 * BLK, width), bf16)] * 4
        + [((4, 2 * BLK, width), f32), ((2 * BLK, width), bf16), ((8, BLK), f32)],
        (pos, names, q, lse, att, cot, lq, lk, glin, pairs_t, mix_t, local, *ex, *ez, *far, k4, v4, prev),
        [SM, SM] + [VM] * 22 + [AN] * 7,
        pool_scratch
        + [pltpu.VMEM((POOL, 2 * BLK, width), f32), pltpu.VMEM((512, width), bf16), pltpu.VMEM((8, BLK), f32)]
        + sems,
    )
    dlk, dq = outs[0], outs[1]
    far_out, own, back, gg = outs[2:6], outs[6], outs[7], outs[8]
    back = lax.ppermute(back, seq, [(i + 1, i) for i in range(NZ * NX - 1)])
    got = [far_out[0]] + [turn(far_out[j], "x", NX, -j) for j in range(1, NX)]
    folded = call(fold_kernel, [((2 * BLK, width), bf16)] * NZ, tuple(got), [VM] * 4)
    ends = [folded[0]] + [turn(folded[i], "z", NZ, -i) for i in range(1, NZ)]
    gk, gv = call(
        finish_kernel,
        [((512, width), bf16), ((512, width), bf16)],
        (pos, key_block, own, back, *ends),
        [SM] + [VM] * 11,
    )
    lead = lambda a: a[None]
    return (lead(mixed), lead(dq), lead(gk), lead(gv), lead(dlq), lead(dlk), gg[0:1])


def solution(mesh):
    grid = Mesh(mesh.devices.reshape(NZ, NX, NY, NC), ("z", "x", "y", "c"))
    cut = P(("y", "c"), ("z", "x"), None)
    flat = P(("y", "c"), None)
    return jax.shard_map(
        per_device,
        mesh=grid,
        in_specs=(cut, cut, cut, cut, cut, flat, cut, P()),
        out_specs=(cut, cut, cut, cut, cut, cut, flat),
        check_vma=False,
    )
```

```python
import functools

import jax
import jax.numpy as jnp
from jax import lax
from jax.experimental import pallas as pl
from jax.experimental.pallas import tpu as pltpu
from jax.sharding import Mesh, PartitionSpec as P


BLK = 128
NZ, NX, NY, NC = 8, 4, 4, 2
masked_value = -1e30
eps_norm = 1e-05
f32 = jnp.float32
bf16 = jnp.bfloat16
NT = (((1,), (1,)), ((), ()))
TN = (((0,), (0,)), ((), ()))
VM = pl.BlockSpec(memory_space=pltpu.VMEM)
SM = pl.BlockSpec(memory_space=pltpu.SMEM)
AN = pl.BlockSpec(memory_space=pl.ANY)
HB = pl.BlockSpec(memory_space=pltpu.HBM)
FAR = NZ * NX
OWN = FAR
PREV = FAR + 4
HALF = 64
TOP = 192
SENT = 144
POOL = FAR + 5


def mm(a, b, dims=None):
    if dims is None:
        return jnp.dot(a, b, preferred_element_type=f32)
    return lax.dot_general(a, b, dims, preferred_element_type=f32)


def call(body, outs, ins, specs, scratch=(), out_specs=None):
    return pl.pallas_call(
        body,
        out_shape=[jax.ShapeDtypeStruct(s, d) for s, d in outs],
        in_specs=list(specs),
        out_specs=out_specs or [VM] * len(outs),
        scratch_shapes=list(scratch),
        compiler_params=pltpu.CompilerParams(vmem_limit_bytes=40 << 20),
    )(*ins)


def rows(b):
    return pl.ds(b * BLK, BLK)


def as_row(col):
    return jnp.broadcast_to(col, (BLK, BLK)).T[0:1]


def as_cols(row):
    return jnp.broadcast_to(row, (BLK, BLK)).T


def lower_mask():
    return lax.broadcasted_iota(jnp.int32, (BLK, BLK), 0) >= lax.broadcasted_iota(
        jnp.int32, (BLK, BLK), 1
    )


def chosen_block(pos, names):
    base = pos[0] * 16 + pos[1] * 4
    far = names[...]
    col = lax.broadcasted_iota(jnp.int32, far.shape, 1)
    hit = (col >= 2) & (far >= base) & (far < base + 4)
    return jnp.max(jnp.where(hit, far - base, 0).astype(f32)).astype(jnp.int32)


def pick_kernel(pos, names, k, v, top, low, last, sems):
    mine = chosen_block(pos, names)
    pairs = [
        (v.at[mine, pl.ds(HALF, HALF)], low),
        (k.at[3], last.at[pl.ds(0, BLK)]),
        (v.at[3], last.at[pl.ds(BLK, BLK)]),
    ]
    for i in range(NZ):
        pairs.append((k.at[mine], top.at[i, pl.ds(0, BLK)]))
        pairs.append((v.at[mine, pl.ds(0, HALF)], top.at[i, pl.ds(BLK, HALF)]))
    copies = [pltpu.make_async_copy(a, b, sems.at[i]) for i, (a, b) in enumerate(pairs)]
    for c in copies:
        c.start()
    for c in copies:
        c.wait()


def place_of(pos, names, b, j):
    name = names[b, j]
    base = pos[0] * 16 + pos[1] * 4
    live = name >= 0
    if j == 0:
        return OWN + b, live
    if j == 1:
        place = jnp.where(name >= base, OWN + name - base, PREV)
        return jnp.where(live, place, OWN), live
    back_x = jnp.bitwise_and(pos[1] - jnp.bitwise_and(jnp.right_shift(name, 2), 3), NX - 1)
    return jnp.where(live, back_x * NZ + jnp.right_shift(name, 4), OWN), live


def pool_copies(far, low, k, v, prev, pool, sems):
    pairs = [(f, pool.at[pl.ds(NZ * j, NZ), pl.ds(0, TOP)]) for j, f in enumerate(far)]
    pairs += [
        (low.at[:, j], pool.at[pl.ds(NZ * j, NZ), pl.ds(TOP, HALF)]) for j in range(NX)
    ]
    pairs += [
        (k, pool.at[pl.ds(OWN, 4), pl.ds(0, BLK)]),
        (v, pool.at[pl.ds(OWN, 4), pl.ds(BLK, BLK)]),
        (prev, pool.at[PREV]),
    ]
    copies = [pltpu.make_async_copy(a, b, sems.at[i]) for i, (a, b) in enumerate(pairs)]
    for c in copies:
        c.start()
    for c in copies:
        c.wait()


GROUP = 4


def attend_kernel(pos, names, q, lk, f0, f1, f2, f3, low, k, v, prev, att, lse, state, pool, s_scr, sems):
    pool_copies((f0, f1, f2, f3), low, k, v, prev, pool, sems)
    nsel = names.shape[1]
    scale = BLK ** (-0.5)

    def block(b, carry):
        qb = q[rows(b), :]
        top = None
        for g in range(0, nsel, GROUP):
            spots = [place_of(pos, names, b, j) for j in range(g, g + GROUP)]
            keys = jnp.concatenate([pool[p, 0:BLK, :] for p, _ in spots], axis=0)
            s = mm(qb, keys, NT)
            for i, (_, live) in enumerate(spots):
                j = g + i
                piece = s[:, i * BLK : (i + 1) * BLK] * scale + jnp.where(live, 0.0, masked_value)
                if j == 0:
                    piece = jnp.where(lower_mask(), piece, masked_value)
                s_scr[:, j * BLK : (j + 1) * BLK] = piece
                top = piece if top is None else jnp.maximum(top, piece)
        row_max = jnp.max(top, axis=1, keepdims=True)
        part = jnp.zeros((BLK, BLK), f32)
        acc = jnp.zeros((BLK, BLK), f32)
        for g in range(0, nsel, GROUP):
            w = jnp.exp(s_scr[:, g * BLK : (g + GROUP) * BLK] - row_max)
            for i in range(GROUP):
                part = part + w[:, i * BLK : (i + 1) * BLK]
            vals = jnp.concatenate(
                [pool[place_of(pos, names, b, j)[0], BLK:, :] for j in range(g, g + GROUP)], axis=0
            )
            acc = acc + mm(w.astype(bf16), vals)
        total = jnp.sum(part, axis=1, keepdims=True)
        att[rows(b), :] = (acc / total).astype(bf16)
        lse[pl.ds(b, 1), :] = as_row(row_max + jnp.log(total))
        return carry

    lax.fori_loop(0, 4, block, 0)
    state[...] = mm(lk[...], att[...], TN).astype(bf16)


def row_kernel(x0, x1, x2, x3, out):
    total = x0[...].astype(f32)
    for r in (x1, x2, x3):
        total = total + r[...].astype(f32)
    total = total.astype(bf16)
    for i in range(NZ):
        out[i] = total


def linear_kernel(pos, lq, lk, att, gain, cot, x0, x1, x2, x3, zs, lin, prior, sums):
    lower = lower_mask()
    run = jnp.zeros((BLK, BLK), f32)
    for j, r in enumerate((x1, x2, x3)):
        run = run + jnp.where(pos[1] > j, r[...].astype(f32), 0.0)
    for i in range(NZ - 1):
        run = run + jnp.where(pos[0] > i, zs[i].astype(f32), 0.0)
    sums[...] = jnp.zeros((8, BLK), f32)
    for b in range(4):
        r = slice(b * BLK, (b + 1) * BLK)
        before = run.astype(bf16)
        prior[b] = before
        mixing = jnp.where(lower, mm(lq[r], lk[r], NT), 0.0).astype(bf16)
        out = mm(mixing, att[r]) + mm(lq[r], before)
        lin[r] = out
        if b < 3:
            run = run + mm(lk[r], att[r], TN)
        scaled = cot[r].astype(f32) * gain[...]
        sums[b : b + 1] = as_row(jnp.sum(out * out, axis=1, keepdims=True))
        sums[4 + b : 5 + b] = as_row(jnp.sum(out * scaled, axis=1, keepdims=True))


def norm_terms(sums, features):
    inv = lax.rsqrt(sums[0:4] / features + eps_norm)
    return inv, inv * inv * inv * sums[4:8] / features


def split_row(row):
    high = row.astype(bf16)
    return high, (row - high.astype(f32)).astype(bf16)


def norm_kernel(features, lq, lin, gain, cot, s0, s1, s2, s3, glin, inv_out, send, local):
    inv, pull = norm_terms(s0[...] + s1[...] + s2[...] + s3[...], features)
    inv_out[0:4] = inv
    inv_out[4:8] = inv
    ggain = jnp.zeros((1, BLK), f32)
    for b in range(4):
        r = slice(b * BLK, (b + 1) * BLK)
        c = cot[r].astype(f32)
        out = lin[r]
        invc = as_cols(inv[b : b + 1])
        ggain = ggain + jnp.sum(c * (out * invc), axis=0, keepdims=True)
        glin[r] = (invc * (c * gain[...]) - out * as_cols(pull[b : b + 1])).astype(bf16)
    run = jnp.zeros((BLK, BLK), f32)
    for b in range(3, -1, -1):
        r = slice(b * BLK, (b + 1) * BLK)
        local[b] = run
        run = run + mm(lq[r], glin[r], TN)
    send[0:BLK] = run.astype(bf16)
    high, rest = split_row(ggain)
    send[BLK : BLK + 8] = jnp.broadcast_to(high, (8, BLK))
    send[BLK + 8 :] = jnp.broadcast_to(rest, (8, BLK))


def sent_kernel(x0, x1, x2, x3, out):
    total = x0[...].astype(f32)
    for r in (x1, x2, x3):
        total = total + r[...].astype(f32)
    high, rest = split_row(total[BLK : BLK + 8] + total[BLK + 8 :])
    state = total[0:BLK].astype(bf16)
    for i in range(NZ):
        out[i, 0:BLK] = state
        out[i, BLK : BLK + 8] = high
        out[i, BLK + 8 :] = rest


def side_kernel(inv, lin, gain, att, glin, lk, lq, prior, mixed, dlq, pairs_t, mix_t):
    lower = lower_mask()
    upper = lax.broadcasted_iota(jnp.int32, (BLK, BLK), 0) <= lax.broadcasted_iota(
        jnp.int32, (BLK, BLK), 1
    )
    for b in range(4):
        r = slice(b * BLK, (b + 1) * BLK)
        normed = lin[r] * as_cols(inv[b : b + 1])
        mixed[r] = (att[r].astype(f32) + gain[...] * normed).astype(bf16)
        pairs = jnp.where(lower, mm(glin[r], att[r], NT), 0.0).astype(bf16)
        dlq[r] = (mm(pairs, lk[r]) + mm(glin[r], prior[b], NT)).astype(bf16)
        pairs_t[b] = jnp.where(upper, mm(att[r], glin[r], NT), 0.0).astype(bf16)
        mix_t[b] = jnp.where(upper, mm(lk[r], lq[r], NT), 0.0).astype(bf16)


def backward_kernel(pos, names, q, lse, att, cot, lq, lk, glin, pairs_t, mix_t, local,
                    x0, x1, x2, x3, zs, f0, f1, f2, f3, low, k, v, prev,
                    dlk, dq, o0, o1, o2, o3, olow, own, back, ggain, pool, acc, gatt, delta, sems):
    pool_copies((f0, f1, f2, f3), low, k, v, prev, pool, sems)
    nsel = names.shape[1]
    scale = BLK ** (-0.5)
    later = jnp.zeros((BLK, BLK), f32)
    for j, r in enumerate((x1, x2, x3)):
        later = later + jnp.where(pos[1] + j + 1 < NX, r[0:BLK].astype(f32), 0.0)
    gg = jnp.zeros((8, BLK), f32)
    for i in range(NZ):
        later = later + jnp.where(pos[0] < i, zs[i, 0:BLK].astype(f32), 0.0)
        gg = gg + zs[i, BLK : BLK + 8].astype(f32) + zs[i, BLK + 8 :].astype(f32)
    ggain[...] = gg
    for b in range(4):
        r = slice(b * BLK, (b + 1) * BLK)
        after = (later + local[b]).astype(bf16)
        dlk[r] = (mm(pairs_t[b], lq[r]) + mm(att[r], after, NT)).astype(bf16)
        g = cot[r].astype(f32) + mm(mix_t[b], glin[r]) + mm(lk[r], after)
        g = g.astype(bf16)
        gatt[r] = g
        delta[b : b + 1] = as_row(
            jnp.sum(g.astype(f32) * att[r].astype(f32), axis=1, keepdims=True)
        )
    acc[...] = jnp.zeros(acc.shape, f32)

    def block(b, carry):
        qb = q[rows(b), :]
        gb = gatt[rows(b), :]
        lse_b = lse[pl.ds(b, 1), :]
        delta_b = delta[pl.ds(b, 1), :]
        dqb = jnp.zeros((BLK, BLK), f32)
        for g in range(0, nsel, GROUP):
            spots = [place_of(pos, names, b, j) for j in range(g, g + GROUP)]
            keys = jnp.concatenate([pool[p, 0:BLK, :] for p, _ in spots], axis=0)
            vals = jnp.concatenate([pool[p, BLK:, :] for p, _ in spots], axis=0)
            s = mm(keys, qb, NT)
            dp = mm(vals, gb, NT)
            pieces = []
            for i, (_, live) in enumerate(spots):
                r = slice(i * BLK, (i + 1) * BLK)
                piece = s[r] * scale + jnp.where(live, 0.0, masked_value)
                if g + i == 0:
                    keep = lax.broadcasted_iota(jnp.int32, (BLK, BLK), 0) <= lax.broadcasted_iota(
                        jnp.int32, (BLK, BLK), 1
                    )
                    piece = jnp.where(keep, piece, masked_value)
                pieces.append(jnp.exp(piece - lse_b))
            p = jnp.concatenate(pieces, axis=0)
            ds = (p * (dp - delta_b)).astype(bf16)
            dv = mm(p.astype(bf16), gb)
            dk = mm(ds, qb)
            dqb = dqb + mm(ds, keys, TN)
            for i, (spot, _) in enumerate(spots):
                r = slice(i * BLK, (i + 1) * BLK)
                acc[spot, 0:BLK, :] += dk[r]
                acc[spot, BLK:, :] += dv[r]
        dq[rows(b), :] = (dqb * scale).astype(bf16)
        return carry

    lax.fori_loop(0, 4, block, 0)
    for j, o in enumerate((o0, o1, o2, o3)):
        o[:, 0:BLK, :] = (acc[NZ * j : NZ * (j + 1), 0:BLK, :] * scale).astype(bf16)
        o[:, BLK:, :] = acc[NZ * j : NZ * (j + 1), BLK:TOP, :].astype(bf16)
        olow[:, j] = acc[NZ * j : NZ * (j + 1), TOP:, :].astype(bf16)
    own[:, 0:BLK, :] = acc[OWN : OWN + 4, 0:BLK, :] * scale
    own[:, BLK:, :] = acc[OWN : OWN + 4, BLK:, :]
    back[0:BLK] = (acc[PREV, 0:BLK, :] * scale).astype(bf16)
    back[BLK:] = acc[PREV, BLK:, :].astype(bf16)


def fold_kernel(a0, a1, a2, a3, low, top, l0, l1, l2, l3):
    total = a0[...].astype(f32) + a1[...].astype(f32) + a2[...].astype(f32) + a3[...].astype(f32)
    top[...] = total.astype(bf16)
    for j, o in enumerate((l0, l1, l2, l3)):
        part = low[0, j].astype(f32)
        for i in range(1, NZ):
            part = part + low[i, j].astype(f32)
        o[...] = part.astype(bf16)


def finish_kernel(pos, names, own, back, top, l0, l1, l2, l3, gk, gv):
    mine = chosen_block(pos, names)
    total = top[0].astype(f32)
    for i in range(1, NZ):
        total = total + top[i].astype(f32)
    part = l0[...].astype(f32) + l1[...].astype(f32) + l2[...].astype(f32) + l3[...].astype(f32)
    gathered = jnp.concatenate([total, part], axis=0)
    for b in range(4):
        whole = own[b] + jnp.where(mine == b, gathered, 0.0)
        if b == 3:
            whole = whole + back[...].astype(f32)
        gk[b * BLK : (b + 1) * BLK] = whole[0:BLK].astype(bf16)
        gv[b * BLK : (b + 1) * BLK] = whole[BLK:].astype(bf16)


def turn(value, axis, size, by):
    return lax.ppermute(value, axis, [(i, (i + by) % size) for i in range(size)])


def swap(value):
    return lax.all_to_all(value, "z", 0, 0, tiled=True)


def turns(values, sign):
    out = []
    for j, value in enumerate(values):
        out.append(turn(value, "x", NX, sign * (j + 1)))
    return out


def per_device(query, key, value, lin_query, lin_key, gain, cotangent, key_block):
    q, k, v, lq, lk, cot = (a[0] for a in (query, key, value, lin_query, lin_key, cotangent))
    width = q.shape[1]
    seq = ("z", "x")
    zi = lax.axis_index("z")
    xi = lax.axis_index("x")
    pos = jnp.stack([zi, xi]).astype(jnp.int32)
    features = float(NY * NC * width)
    names = lax.dynamic_slice_in_dim(key_block, (zi * NX + xi) * 4, 4, 0)
    k4 = k.reshape(4, BLK, width)
    v4 = v.reshape(4, BLK, width)
    tile = (BLK, BLK)

    tops, low, last = call(
        pick_kernel,
        [((NZ, TOP, width), bf16), ((HALF, width), bf16), ((2 * BLK, width), bf16)],
        (pos, key_block, k4, v4),
        [SM, VM, HB, HB],
        [pltpu.SemaphoreType.DMA((2 * NZ + 3,))],
        [HB, VM, VM],
    )
    prev = lax.ppermute(last, seq, [(i, i + 1) for i in range(NZ * NX - 1)])
    lows = jnp.stack([low] + [turn(low, "x", NX, j) for j in range(1, NX)])
    tops = swap(tops)
    lows = jnp.broadcast_to(lows[None], (NZ, NX, HALF, width))
    tops, lows, prev = lax.optimization_barrier((tops, lows, prev))
    far = [tops] + turns([tops] * 3, 1)
    lows = swap(lows)

    pool_scratch = [pltpu.VMEM((POOL, 2 * BLK, width), bf16)]
    sems = [pltpu.SemaphoreType.DMA((2 * NX + 3,))]
    att, lse, state = call(
        attend_kernel,
        [((512, width), bf16), ((8, BLK), f32), (tile, bf16)],
        (pos, names, q, lk, *far, lows, k4, v4, prev),
        [SM, SM, VM, VM] + [AN] * 8,
        pool_scratch + [pltpu.VMEM((BLK, names.shape[1] * BLK), f32)] + sems,
    )

    xs = [state] + [turn(state, "x", NX, j) for j in range(1, NX)]
    (wide,) = call(row_kernel, [((NZ, BLK, width), bf16)], xs, [VM] * 4)
    lin, prior, sums = call(
        linear_kernel,
        [((512, width), f32), ((4, BLK, width), bf16), ((8, BLK), f32)],
        (pos, lq, lk, att, gain, cot, *xs, swap(wide)),
        [SM] + [VM] * 10,
    )
    sums = sums + turn(sums, "c", NC, 1)
    ys = [sums] + [turn(sums, "y", NY, i) for i in range(1, NY)]
    glin, inv, send, local = call(
        functools.partial(norm_kernel, features),
        [((512, width), bf16), ((8, BLK), f32), ((SENT, BLK), bf16), ((4, BLK, BLK), f32)],
        (lq, lin, gain, cot, *ys),
        [VM] * 8,
    )
    ex = [send] + [turn(send, "x", NX, -j) for j in range(1, NX)]
    mixed, dlq, pairs_t, mix_t = call(
        side_kernel,
        [((512, width), bf16), ((512, width), bf16), ((4, BLK, BLK), bf16), ((4, BLK, BLK), bf16)],
        (inv, lin, gain, att, glin, lk, lq, prior),
        [VM] * 8,
    )
    *ex, mixed, dlq, pairs_t, mix_t = lax.optimization_barrier((*ex, mixed, dlq, pairs_t, mix_t))
    (wide,) = call(sent_kernel, [((NZ, SENT, width), bf16)], ex, [VM] * 4)
    outs = call(
        backward_kernel,
        [((512, width), bf16), ((512, width), bf16)]
        + [((NZ, TOP, width), bf16)] * 4
        + [((NZ, NX, HALF, width), bf16), ((4, 2 * BLK, width), f32)]
        + [((2 * BLK, width), bf16), ((8, BLK), f32)],
        (pos, names, q, lse, att, cot, lq, lk, glin, pairs_t, mix_t, local, *ex, swap(wide))
        + (*far, lows, k4, v4, prev),
        [SM, SM] + [VM] * 15 + [AN] * 8,
        pool_scratch
        + [pltpu.VMEM((POOL, 2 * BLK, width), f32), pltpu.VMEM((512, width), bf16), pltpu.VMEM((8, BLK), f32)]
        + sems,
    )
    dlk, dq = outs[0], outs[1]
    far_out, low_out, own, back, gg = outs[2:6], outs[6], outs[7], outs[8], outs[9]
    back = lax.ppermute(back, seq, [(i + 1, i) for i in range(NZ * NX - 1)])
    got = [far_out[0]] + turns(far_out[1:], -1)
    folded = call(
        fold_kernel,
        [((NZ, TOP, width), bf16)] + [((HALF, width), bf16)] * NX,
        (*got, swap(low_out)),
        [VM] * 5,
    )
    ends = [folded[1]] + turns(folded[2:], -1)
    gk, gv = call(
        finish_kernel,
        [((512, width), bf16), ((512, width), bf16)],
        (pos, key_block, own, back, swap(folded[0]), *ends),
        [SM] + [VM] * 8,
    )
    lead = lambda a: a[None]
    return (lead(mixed), lead(dq), lead(gk), lead(gv), lead(dlq), lead(dlk), gg[0:1])


def solution(mesh):
    grid = Mesh(mesh.devices.reshape(NZ, NX, NY, NC), ("z", "x", "y", "c"))
    cut = P(("y", "c"), ("z", "x"), None)
    flat = P(("y", "c"), None)
    return jax.shard_map(
        per_device,
        mesh=grid,
        in_specs=(cut, cut, cut, cut, cut, flat, cut, P()),
        out_specs=(cut, cut, cut, cut, cut, cut, flat),
        check_vma=False,
    )
```

```python
import functools

import jax
import jax.numpy as jnp
from jax import lax
from jax.experimental import pallas as pl
from jax.experimental.pallas import tpu as pltpu
from jax.sharding import Mesh, PartitionSpec as P


BLK = 128
NZ, NX, NY, NC = 8, 4, 4, 2
masked_value = -1e30
eps_norm = 1e-05
f32 = jnp.float32
bf16 = jnp.bfloat16
NT = (((1,), (1,)), ((), ()))
TN = (((0,), (0,)), ((), ()))
VM = pl.BlockSpec(memory_space=pltpu.VMEM)
SM = pl.BlockSpec(memory_space=pltpu.SMEM)
AN = pl.BlockSpec(memory_space=pl.ANY)
HB = pl.BlockSpec(memory_space=pltpu.HBM)
FAR = NZ * NX
OWN = FAR
PREV = FAR + 4
HALF = 64
TOP = 192
SENT = 144
POOL = FAR + 5


def mm(a, b, dims=None):
    if dims is None:
        return jnp.dot(a, b, preferred_element_type=f32)
    return lax.dot_general(a, b, dims, preferred_element_type=f32)


def call(body, outs, ins, specs, scratch=(), out_specs=None, vmem=8):
    return pl.pallas_call(
        body,
        out_shape=[jax.ShapeDtypeStruct(s, d) for s, d in outs],
        in_specs=list(specs),
        out_specs=out_specs or [VM] * len(outs),
        scratch_shapes=list(scratch),
        compiler_params=pltpu.CompilerParams(vmem_limit_bytes=vmem << 20),
    )(*ins)


def rows(b):
    return pl.ds(b * BLK, BLK)


def as_row(col):
    return jnp.broadcast_to(col, (BLK, BLK)).T[0:1]


def as_cols(row):
    return jnp.broadcast_to(row, (BLK, BLK)).T


def lower_mask():
    return lax.broadcasted_iota(jnp.int32, (BLK, BLK), 0) >= lax.broadcasted_iota(
        jnp.int32, (BLK, BLK), 1
    )


def chosen_block(pos, names):
    base = pos[0] * 16 + pos[1] * 4
    far = names[...]
    col = lax.broadcasted_iota(jnp.int32, far.shape, 1)
    hit = (col >= 2) & (far >= base) & (far < base + 4)
    return jnp.max(jnp.where(hit, far - base, 0).astype(f32)).astype(jnp.int32)


def pick_kernel(pos, names, k, v, top, low, last, sems):
    mine = chosen_block(pos, names)
    pairs = [
        (v.at[mine, pl.ds(HALF, HALF)], low),
        (k.at[3], last.at[:, pl.ds(0, BLK)]),
        (v.at[3], last.at[:, pl.ds(BLK, BLK)]),
    ]
    for i in range(NZ):
        pairs.append((k.at[mine], top.at[i, pl.ds(0, BLK)]))
        pairs.append((v.at[mine, pl.ds(0, HALF)], top.at[i, pl.ds(BLK, HALF)]))
    run_copies(pairs, sems)


def place_of(pos, names, b, j):
    name = names[b, j]
    base = pos[0] * 16 + pos[1] * 4
    live = name >= 0
    if j == 0:
        return OWN + b, live
    if j == 1:
        place = jnp.where(name >= base, OWN + name - base, PREV)
        return jnp.where(live, place, OWN), live
    back_x = jnp.bitwise_and(pos[1] - jnp.bitwise_and(jnp.right_shift(name, 2), 3), NX - 1)
    return jnp.where(live, back_x * NZ + jnp.right_shift(name, 4), OWN), live


def run_copies(pairs, sems):
    copies = [pltpu.make_async_copy(a, b, sems.at[i]) for i, (a, b) in enumerate(pairs)]
    for c in copies:
        c.start()
    for c in copies:
        c.wait()


def pool_pairs(far, low, k, v, prev, pool):
    left, right = pl.ds(0, BLK), pl.ds(BLK, BLK)
    pairs = [(prev, pool.at[PREV])]
    pairs.append((k, pool.at[pl.ds(OWN, 4), :, left]))
    pairs.append((v, pool.at[pl.ds(OWN, 4), :, right]))
    for j, f in enumerate(far):
        spot = pl.ds(NZ * j, NZ)
        pairs.append((f.at[:, pl.ds(0, BLK)], pool.at[spot, :, left]))
        pairs.append((f.at[:, pl.ds(BLK, HALF)], pool.at[spot, pl.ds(0, HALF), right]))
        pairs.append((low.at[:, j], pool.at[spot, pl.ds(HALF, HALF), right]))
    return pairs


GROUP = 4


def attend_kernel(pos, names, q, lk, f0, f1, f2, f3, low, k, v, prev, att, lse, state, pool, s_scr, sems):
    run_copies(pool_pairs((f0, f1, f2, f3), low, k, v, prev, pool), sems)
    nsel = names.shape[1]
    scale = BLK ** (-0.5)

    def block(b, carry):
        qb = q[rows(b), :]
        top = None
        for g in range(0, nsel, GROUP):
            spots = [place_of(pos, names, b, j) for j in range(g, g + GROUP)]
            keys = jnp.concatenate([pool[p, :, 0:BLK] for p, _ in spots], axis=0)
            s = mm(qb, keys, NT)
            for i, (_, live) in enumerate(spots):
                j = g + i
                piece = s[:, i * BLK : (i + 1) * BLK] * scale + jnp.where(live, 0.0, masked_value)
                if j == 0:
                    piece = jnp.where(lower_mask(), piece, masked_value)
                s_scr[:, j * BLK : (j + 1) * BLK] = piece
                top = piece if top is None else jnp.maximum(top, piece)
        row_max = jnp.max(top, axis=1, keepdims=True)
        part = jnp.zeros((BLK, BLK), f32)
        acc = jnp.zeros((BLK, BLK), f32)
        for g in range(0, nsel, GROUP):
            w = jnp.exp(s_scr[:, g * BLK : (g + GROUP) * BLK] - row_max)
            for i in range(GROUP):
                part = part + w[:, i * BLK : (i + 1) * BLK]
            vals = jnp.concatenate(
                [pool[place_of(pos, names, b, j)[0], :, BLK:] for j in range(g, g + GROUP)], axis=0
            )
            acc = acc + mm(w.astype(bf16), vals)
        total = jnp.sum(part, axis=1, keepdims=True)
        att[rows(b), :] = (acc / total).astype(bf16)
        lse[pl.ds(b, 1), :] = as_row(row_max + jnp.log(total))
        return carry

    lax.fori_loop(0, 4, block, 0)
    state[...] = mm(lk[...], att[...], TN).astype(bf16)


def row_kernel(x0, x1, x2, x3, out):
    total = x0[...].astype(f32)
    for r in (x1, x2, x3):
        total = total + r[...].astype(f32)
    total = total.astype(bf16)
    for i in range(NZ):
        out[i] = total


def spread_kernel(l0, l1, l2, l3, out, block, sems):
    for j, r in enumerate((l0, l1, l2, l3)):
        block[j] = r[...]
    run_copies([(block, out.at[i]) for i in range(NZ)], sems)


def linear_kernel(pos, lq, lk, att, gain, cot, x0, x1, x2, x3, zs, lin, prior, sums):
    lower = lower_mask()
    run = jnp.zeros((BLK, BLK), f32)
    for j, r in enumerate((x1, x2, x3)):
        run = run + jnp.where(pos[1] > j, r[...].astype(f32), 0.0)
    for i in range(NZ - 1):
        run = run + jnp.where(pos[0] > i, zs[i].astype(f32), 0.0)
    sums[...] = jnp.zeros((8, BLK), f32)
    for b in range(4):
        r = slice(b * BLK, (b + 1) * BLK)
        before = run.astype(bf16)
        prior[b] = before
        mixing = jnp.where(lower, mm(lq[r], lk[r], NT), 0.0).astype(bf16)
        out = mm(mixing, att[r]) + mm(lq[r], before)
        lin[r] = out
        if b < 3:
            run = run + mm(lk[r], att[r], TN)
        scaled = cot[r].astype(f32) * gain[...]
        sums[b : b + 1] = as_row(jnp.sum(out * out, axis=1, keepdims=True))
        sums[4 + b : 5 + b] = as_row(jnp.sum(out * scaled, axis=1, keepdims=True))


def norm_terms(sums, features):
    inv = lax.rsqrt(sums[0:4] / features + eps_norm)
    return inv, inv * inv * inv * sums[4:8] / features


def split_row(row):
    high = row.astype(bf16)
    return high, (row - high.astype(f32)).astype(bf16)


def norm_kernel(features, lq, lin, gain, cot, s0, s1, s2, s3, glin, inv_out, send, local):
    inv, pull = norm_terms(s0[...] + s1[...] + s2[...] + s3[...], features)
    inv_out[0:4] = inv
    inv_out[4:8] = inv
    ggain = jnp.zeros((1, BLK), f32)
    for b in range(4):
        r = slice(b * BLK, (b + 1) * BLK)
        c = cot[r].astype(f32)
        out = lin[r]
        invc = as_cols(inv[b : b + 1])
        ggain = ggain + jnp.sum(c * (out * invc), axis=0, keepdims=True)
        glin[r] = (invc * (c * gain[...]) - out * as_cols(pull[b : b + 1])).astype(bf16)
    run = jnp.zeros((BLK, BLK), f32)
    for b in range(3, -1, -1):
        r = slice(b * BLK, (b + 1) * BLK)
        local[b] = run
        run = run + mm(lq[r], glin[r], TN)
    send[0:BLK] = run.astype(bf16)
    high, rest = split_row(ggain)
    send[BLK : BLK + 8] = jnp.broadcast_to(high, (8, BLK))
    send[BLK + 8 :] = jnp.broadcast_to(rest, (8, BLK))


def sent_kernel(x0, x1, x2, x3, out):
    total = x0[...].astype(f32)
    for r in (x1, x2, x3):
        total = total + r[...].astype(f32)
    high, rest = split_row(total[BLK : BLK + 8] + total[BLK + 8 :])
    state = total[0:BLK].astype(bf16)
    for i in range(NZ):
        out[i, 0:BLK] = state
        out[i, BLK : BLK + 8] = high
        out[i, BLK + 8 :] = rest


def side_kernel(inv, lin, gain, att, glin, lk, lq, prior, mixed, dlq, pairs_t, mix_t):
    lower = lower_mask()
    upper = lax.broadcasted_iota(jnp.int32, (BLK, BLK), 0) <= lax.broadcasted_iota(
        jnp.int32, (BLK, BLK), 1
    )
    for b in range(4):
        r = slice(b * BLK, (b + 1) * BLK)
        normed = lin[r] * as_cols(inv[b : b + 1])
        mixed[r] = (att[r].astype(f32) + gain[...] * normed).astype(bf16)
        pairs = jnp.where(lower, mm(glin[r], att[r], NT), 0.0).astype(bf16)
        dlq[r] = (mm(pairs, lk[r]) + mm(glin[r], prior[b], NT)).astype(bf16)
        pairs_t[b] = jnp.where(upper, mm(att[r], glin[r], NT), 0.0).astype(bf16)
        mix_t[b] = jnp.where(upper, mm(lk[r], lq[r], NT), 0.0).astype(bf16)


def backward_kernel(pos, names, q, lse, att, cot, lq, lk, glin, pairs_t, mix_t, local,
                    x0, x1, x2, x3, zs, pool,
                    dlk, dq, o0, o1, o2, o3, olow, own, back, ggain,
                    acc, gatt, delta, near, lows, sems):
    nsel = names.shape[1]
    scale = BLK ** (-0.5)
    later = jnp.zeros((BLK, BLK), f32)
    for j, r in enumerate((x1, x2, x3)):
        later = later + jnp.where(pos[1] + j + 1 < NX, r[0:BLK].astype(f32), 0.0)
    gg = jnp.zeros((8, BLK), f32)
    for i in range(NZ):
        later = later + jnp.where(pos[0] < i, zs[i, 0:BLK].astype(f32), 0.0)
        gg = gg + zs[i, BLK : BLK + 8].astype(f32) + zs[i, BLK + 8 :].astype(f32)
    ggain[...] = gg
    for b in range(4):
        r = slice(b * BLK, (b + 1) * BLK)
        after = (later + local[b]).astype(bf16)
        dlk[r] = (mm(pairs_t[b], lq[r]) + mm(att[r], after, NT)).astype(bf16)
        g = cot[r].astype(f32) + mm(mix_t[b], glin[r]) + mm(lk[r], after)
        g = g.astype(bf16)
        gatt[r] = g
        delta[b : b + 1] = as_row(
            jnp.sum(g.astype(f32) * att[r].astype(f32), axis=1, keepdims=True)
        )
    acc[...] = jnp.zeros(acc.shape, f32)

    def block(b, carry):
        qb = q[rows(b), :]
        gb = gatt[rows(b), :]
        lse_b = lse[pl.ds(b, 1), :]
        delta_b = delta[pl.ds(b, 1), :]
        dqb = jnp.zeros((BLK, BLK), f32)
        zero = jnp.zeros((BLK, BLK), bf16)
        both = jnp.concatenate(
            [jnp.concatenate([qb, zero], axis=1), jnp.concatenate([zero, gb], axis=1)], axis=0
        )
        for g in range(0, nsel, GROUP):
            spots = [place_of(pos, names, b, j) for j in range(g, g + GROUP)]
            keyval = jnp.concatenate([pool[p] for p, _ in spots], axis=0)
            sdp = mm(keyval, both, NT)
            pieces = []
            for i, (_, live) in enumerate(spots):
                r = slice(i * BLK, (i + 1) * BLK)
                piece = sdp[r, 0:BLK] * scale + (jnp.where(live, 0.0, masked_value) - lse_b)
                if g + i == 0:
                    keep = lax.broadcasted_iota(jnp.int32, (BLK, BLK), 0) <= lax.broadcasted_iota(
                        jnp.int32, (BLK, BLK), 1
                    )
                    piece = jnp.where(keep, piece, masked_value)
                pieces.append(jnp.exp(piece))
            p = jnp.concatenate(pieces, axis=0)
            ds = (p * (sdp[:, BLK:] - delta_b)).astype(bf16)
            grads = mm(jnp.concatenate([ds, p.astype(bf16)], axis=1), both)
            dqb = dqb + mm(ds, keyval[:, 0:BLK], TN)
            for i, (spot, _) in enumerate(spots):
                acc[spot] += grads[i * BLK : (i + 1) * BLK]
        dq[rows(b), :] = (dqb * scale).astype(bf16)
        return carry

    lax.fori_loop(0, 4, block, 0)
    for j in range(NX):
        lows[:, j] = acc[NZ * j : NZ * (j + 1), HALF:, BLK:].astype(bf16)
    near[:, 0:BLK] = (acc[0:NZ, :, 0:BLK] * scale).astype(bf16)
    near[:, BLK:] = acc[0:NZ, 0:HALF, BLK:].astype(bf16)
    copies = [pltpu.make_async_copy(lows, olow, sems.at[0]), pltpu.make_async_copy(near, o0, sems.at[1])]
    for c in copies:
        c.start()
    for j, o in ((1, o1), (2, o2), (3, o3)):
        o[:, 0:BLK] = (acc[NZ * j : NZ * (j + 1), :, 0:BLK] * scale).astype(bf16)
        o[:, BLK:] = acc[NZ * j : NZ * (j + 1), 0:HALF, BLK:].astype(bf16)
    own[:, :, 0:BLK] = acc[OWN : OWN + 4, :, 0:BLK] * scale
    own[:, :, BLK:] = acc[OWN : OWN + 4, :, BLK:]
    back[:, 0:BLK] = (acc[PREV, :, 0:BLK] * scale).astype(bf16)
    back[:, BLK:] = acc[PREV, :, BLK:].astype(bf16)
    for c in copies:
        c.wait()


def fold_kernel(a0, a1, a2, a3, low, top, l0, l1, l2, l3):
    total = a0[...].astype(f32) + a1[...].astype(f32) + a2[...].astype(f32) + a3[...].astype(f32)
    top[...] = total.astype(bf16)
    for j, o in enumerate((l0, l1, l2, l3)):
        part = low[0, j].astype(f32)
        for i in range(1, NZ):
            part = part + low[i, j].astype(f32)
        o[...] = part.astype(bf16)


def finish_kernel(pos, names, own, back, top, l0, l1, l2, l3, gk, gv):
    mine = chosen_block(pos, names)
    total = top[0].astype(f32)
    for i in range(1, NZ):
        total = total + top[i].astype(f32)
    part = l0[...].astype(f32) + l1[...].astype(f32) + l2[...].astype(f32) + l3[...].astype(f32)
    far_key, far_value = total[0:BLK], jnp.concatenate([total[BLK:], part], axis=0)
    for b in range(4):
        r = slice(b * BLK, (b + 1) * BLK)
        dk = own[b, :, 0:BLK] + jnp.where(mine == b, far_key, 0.0)
        dv = own[b, :, BLK:] + jnp.where(mine == b, far_value, 0.0)
        if b == 3:
            dk = dk + back[:, 0:BLK].astype(f32)
            dv = dv + back[:, BLK:].astype(f32)
        gk[r] = dk.astype(bf16)
        gv[r] = dv.astype(bf16)


def turn(value, axis, size, by):
    return lax.ppermute(value, axis, [(i, (i + by) % size) for i in range(size)])


def in_hbm(value):
    return pltpu.with_memory_space_constraint(value, pltpu.HBM)


def swap(value):
    return lax.all_to_all(value, "z", 0, 0, tiled=True)


def turns(values, sign):
    out = []
    for j, value in enumerate(values):
        out.append(turn(value, "x", NX, sign * (j + 1)))
    return out


def per_device(query, key, value, lin_query, lin_key, gain, cotangent, key_block):
    q, k, v, lq, lk, cot = (a[0] for a in (query, key, value, lin_query, lin_key, cotangent))
    width = q.shape[1]
    seq = ("z", "x")
    zi = lax.axis_index("z")
    xi = lax.axis_index("x")
    pos = jnp.stack([zi, xi]).astype(jnp.int32)
    features = float(NY * NC * width)
    names = lax.dynamic_slice_in_dim(key_block, (zi * NX + xi) * 4, 4, 0)
    k4 = k.reshape(4, BLK, width)
    v4 = v.reshape(4, BLK, width)
    tile = (BLK, BLK)

    tops, low, last = call(
        pick_kernel,
        [((NZ, TOP, width), bf16), ((HALF, width), bf16), ((BLK, 2 * BLK), bf16)],
        (pos, key_block, in_hbm(k4), in_hbm(v4)),
        [SM, VM, HB, HB],
        [pltpu.SemaphoreType.DMA((2 * NZ + 3,))],
        [HB, VM, VM],
    )
    prev = lax.ppermute(last, seq, [(i, i + 1) for i in range(NZ * NX - 1)])
    lows = [low] + [turn(low, "x", NX, j) for j in range(1, NX)]
    (lows,) = call(
        spread_kernel,
        [((NZ, NX, HALF, width), bf16)],
        lows,
        [VM] * 4,
        [pltpu.VMEM((NX, HALF, width), bf16), pltpu.SemaphoreType.DMA((NZ,))],
        [HB],
    )
    tops = swap(tops)
    tops, lows = lax.optimization_barrier((tops, lows))
    far = [tops] + turns([tops] * 3, 1)
    lows = swap(lows)

    att, lse, state, pool = call(
        attend_kernel,
        [((512, width), bf16), ((8, BLK), f32), (tile, bf16), ((POOL, BLK, 2 * BLK), bf16)],
        (pos, names, q, lk, *far, lows, k4, v4, prev),
        [SM, SM, VM, VM] + [AN] * 8,
        [pltpu.VMEM((BLK, names.shape[1] * BLK), f32), pltpu.SemaphoreType.DMA((3 * NX + 3,))],
        vmem=16,
    )

    xs = [state] + [turn(state, "x", NX, j) for j in range(1, NX)]
    (wide,) = call(row_kernel, [((NZ, BLK, width), bf16)], xs, [VM] * 4)
    lin, prior, sums = call(
        linear_kernel,
        [((512, width), f32), ((4, BLK, width), bf16), ((8, BLK), f32)],
        (pos, lq, lk, att, gain, cot, *xs, swap(wide)),
        [SM] + [VM] * 10,
    )
    sums = sums + turn(sums, "c", NC, 1)
    ys = [sums] + [turn(sums, "y", NY, i) for i in range(1, NY)]
    glin, inv, send, local = call(
        functools.partial(norm_kernel, features),
        [((512, width), bf16), ((8, BLK), f32), ((SENT, BLK), bf16), ((4, BLK, BLK), f32)],
        (lq, lin, gain, cot, *ys),
        [VM] * 8,
    )
    ex = [send] + [turn(send, "x", NX, -j) for j in range(1, NX)]
    mixed, dlq, pairs_t, mix_t = call(
        side_kernel,
        [((512, width), bf16), ((512, width), bf16), ((4, BLK, BLK), bf16), ((4, BLK, BLK), bf16)],
        (inv, lin, gain, att, glin, lk, lq, prior),
        [VM] * 8,
    )
    *ex, mixed, dlq, pairs_t, mix_t = lax.optimization_barrier((*ex, mixed, dlq, pairs_t, mix_t))
    (wide,) = call(sent_kernel, [((NZ, SENT, width), bf16)], ex, [VM] * 4)
    outs = call(
        backward_kernel,
        [((512, width), bf16), ((512, width), bf16)]
        + [((NZ, TOP, width), bf16)] * 4
        + [((NZ, NX, HALF, width), bf16), ((4, BLK, 2 * BLK), f32)]
        + [((BLK, 2 * BLK), bf16), ((8, BLK), f32)],
        (pos, names, q, lse, att, cot, lq, lk, glin, pairs_t, mix_t, local, *ex, swap(wide), pool),
        [SM, SM] + [VM] * 16,
        [
            pltpu.VMEM((POOL, BLK, 2 * BLK), f32),
            pltpu.VMEM((512, width), bf16),
            pltpu.VMEM((8, BLK), f32),
            pltpu.VMEM((NZ, TOP, width), bf16),
            pltpu.VMEM((NZ, NX, HALF, width), bf16),
            pltpu.SemaphoreType.DMA((2,)),
        ],
        [VM, VM, HB, VM, VM, VM, HB, VM, VM, VM],
        vmem=24,
    )
    dlk, dq = outs[0], outs[1]
    far_out, low_out, own, back, gg = outs[2:6], outs[6], outs[7], outs[8], outs[9]
    back = lax.ppermute(back, seq, [(i + 1, i) for i in range(NZ * NX - 1)])
    got = [far_out[0]] + turns(far_out[1:], -1)
    folded = call(
        fold_kernel,
        [((NZ, TOP, width), bf16)] + [((HALF, width), bf16)] * NX,
        (*got, swap(low_out)),
        [VM] * 5,
    )
    ends = [folded[1]] + turns(folded[2:], -1)
    gk, gv = call(
        finish_kernel,
        [((512, width), bf16), ((512, width), bf16)],
        (pos, key_block, own, back, swap(folded[0]), *ends),
        [SM] + [VM] * 8,
    )
    lead = lambda a: a[None]
    return (lead(mixed), lead(dq), lead(gk), lead(gv), lead(dlq), lead(dlk), gg[0:1])


def solution(mesh):
    grid = Mesh(mesh.devices.reshape(NZ, NX, NY, NC), ("z", "x", "y", "c"))
    cut = P(("y", "c"), ("z", "x"), None)
    flat = P(("y", "c"), None)
    return jax.shard_map(
        per_device,
        mesh=grid,
        in_specs=(cut, cut, cut, cut, cut, flat, cut, P()),
        out_specs=(cut, cut, cut, cut, cut, cut, flat),
        check_vma=False,
    )
```

```python
import functools

import jax
import jax.numpy as jnp
from jax import lax
from jax.experimental import pallas as pl
from jax.experimental.pallas import tpu as pltpu
from jax.sharding import Mesh, PartitionSpec as P


BLK = 128
NZ, NX, NY, NC = 8, 4, 4, 2
masked_value = -1e30
eps_norm = 1e-05
f32 = jnp.float32
bf16 = jnp.bfloat16
NT = (((1,), (1,)), ((), ()))
TN = (((0,), (0,)), ((), ()))
VM = pl.BlockSpec(memory_space=pltpu.VMEM)
SM = pl.BlockSpec(memory_space=pltpu.SMEM)
AN = pl.BlockSpec(memory_space=pl.ANY)
HB = pl.BlockSpec(memory_space=pltpu.HBM)
FAR = NZ * NX
OWN = FAR
PREV = FAR + 4
HALF = 64
TOP = 192
SENT = 144
POOL = FAR + 5


def mm(a, b, dims=None):
    if dims is None:
        return jnp.dot(a, b, preferred_element_type=f32)
    return lax.dot_general(a, b, dims, preferred_element_type=f32)


def call(body, outs, ins, specs, scratch=(), out_specs=None, vmem=8):
    return pl.pallas_call(
        body,
        out_shape=[jax.ShapeDtypeStruct(s, d) for s, d in outs],
        in_specs=list(specs),
        out_specs=out_specs or [VM] * len(outs),
        scratch_shapes=list(scratch),
        compiler_params=pltpu.CompilerParams(vmem_limit_bytes=vmem << 20),
    )(*ins)


def rows(b):
    return pl.ds(b * BLK, BLK)


def as_row(col):
    return jnp.broadcast_to(col, (BLK, BLK)).T[0:1]


def as_cols(row):
    return jnp.broadcast_to(row, (BLK, BLK)).T


def lower_mask():
    return lax.broadcasted_iota(jnp.int32, (BLK, BLK), 0) >= lax.broadcasted_iota(
        jnp.int32, (BLK, BLK), 1
    )


def chosen_block(pos, names):
    base = pos[0] * 16 + pos[1] * 4
    far = names[...]
    col = lax.broadcasted_iota(jnp.int32, far.shape, 0)
    hit = (col >= 2) & (far >= base) & (far < base + 4)
    return jnp.max(jnp.where(hit, far - base, 0).astype(f32)).astype(jnp.int32)


def pick_kernel(pos, names, k, v, top, low, last, block, sems):
    mine = chosen_block(pos, names)
    run_copies(
        [
            (k.at[mine], block.at[pl.ds(0, BLK)]),
            (v.at[mine, pl.ds(0, HALF)], block.at[pl.ds(BLK, HALF)]),
            (v.at[mine, pl.ds(HALF, HALF)], low),
            (k.at[3], last.at[:, pl.ds(0, BLK)]),
            (v.at[3], last.at[:, pl.ds(BLK, BLK)]),
        ],
        sems,
    )
    run_copies([(block, top.at[i]) for i in range(NZ)], sems)


def place_of(pos, names, b, j):
    name = names[j, b]
    base = pos[0] * 16 + pos[1] * 4
    live = name >= 0
    if j == 0:
        return OWN + b, live
    if j == 1:
        place = jnp.where(name >= base, OWN + name - base, PREV)
        return jnp.where(live, place, OWN), live
    back_x = jnp.bitwise_and(pos[1] - jnp.bitwise_and(jnp.right_shift(name, 2), 3), NX - 1)
    return jnp.where(live, back_x * NZ + jnp.right_shift(name, 4), OWN), live


def run_copies(pairs, sems):
    copies = [pltpu.make_async_copy(a, b, sems.at[i]) for i, (a, b) in enumerate(pairs)]
    for c in copies:
        c.start()
    for c in copies:
        c.wait()


def pool_pairs(far, low, k, v, prev, pool):
    left, right = pl.ds(0, BLK), pl.ds(BLK, BLK)
    pairs = [(prev, pool.at[PREV])]
    pairs.append((k, pool.at[pl.ds(OWN, 4), :, left]))
    pairs.append((v, pool.at[pl.ds(OWN, 4), :, right]))
    for j, f in enumerate(far):
        spot = pl.ds(NZ * j, NZ)
        pairs.append((f.at[:, pl.ds(0, BLK)], pool.at[spot, :, left]))
        pairs.append((f.at[:, pl.ds(BLK, HALF)], pool.at[spot, pl.ds(0, HALF), right]))
        pairs.append((low.at[:, j], pool.at[spot, pl.ds(HALF, HALF), right]))
    return pairs


GROUP = 4
BGROUP = 20


def attend_kernel(pos, names, q, lk, f0, f1, f2, f3, low, k, v, prev, att, lse, state, pool, s_scr, sems):
    run_copies(pool_pairs((f0, f1, f2, f3), low, k, v, prev, pool), sems)
    nsel = names.shape[0]
    scale = BLK ** (-0.5)

    def block(b, carry):
        qb = q[rows(b), :]
        top = None
        for g in range(0, nsel, GROUP):
            spots = [place_of(pos, names, b, j) for j in range(g, g + GROUP)]
            keys = jnp.concatenate([pool[p, :, 0:BLK] for p, _ in spots], axis=0)
            s = mm(qb, keys, NT)
            for i, (_, live) in enumerate(spots):
                j = g + i
                piece = s[:, i * BLK : (i + 1) * BLK] * scale + jnp.where(live, 0.0, masked_value)
                if j == 0:
                    piece = jnp.where(lower_mask(), piece, masked_value)
                s_scr[:, j * BLK : (j + 1) * BLK] = piece
                top = piece if top is None else jnp.maximum(top, piece)
        row_max = jnp.max(top, axis=1, keepdims=True)
        part = jnp.zeros((BLK, BLK), f32)
        acc = jnp.zeros((BLK, BLK), f32)
        for g in range(0, nsel, GROUP):
            w = jnp.exp(s_scr[:, g * BLK : (g + GROUP) * BLK] - row_max)
            for i in range(GROUP):
                part = part + w[:, i * BLK : (i + 1) * BLK]
            vals = jnp.concatenate(
                [pool[place_of(pos, names, b, j)[0], :, BLK:] for j in range(g, g + GROUP)], axis=0
            )
            acc = acc + mm(w.astype(bf16), vals)
        total = jnp.sum(part, axis=1, keepdims=True)
        att[rows(b), :] = (acc / total).astype(bf16)
        lse[pl.ds(b, 1), :] = as_row(row_max + jnp.log(total))
        return carry

    lax.fori_loop(0, 4, block, 0)
    state[...] = mm(lk[...], att[...], TN).astype(bf16)


def row_kernel(x0, x1, x2, x3, out):
    total = x0[...].astype(f32)
    for r in (x1, x2, x3):
        total = total + r[...].astype(f32)
    total = total.astype(bf16)
    for i in range(NZ):
        out[i] = total


def spread_kernel(l0, l1, l2, l3, out, block, sems):
    for j, r in enumerate((l0, l1, l2, l3)):
        block[j] = r[...]
    run_copies([(block, out.at[i]) for i in range(NZ)], sems)


def linear_kernel(pos, lq, lk, att, gain, cot, x0, x1, x2, x3, zs, lin, prior, sums):
    lower = lower_mask()
    run = jnp.zeros((BLK, BLK), f32)
    for j, r in enumerate((x1, x2, x3)):
        run = run + jnp.where(pos[1] > j, r[...].astype(f32), 0.0)
    for i in range(NZ - 1):
        run = run + jnp.where(pos[0] > i, zs[i].astype(f32), 0.0)
    sums[...] = jnp.zeros((8, BLK), f32)
    for b in range(4):
        r = slice(b * BLK, (b + 1) * BLK)
        before = run.astype(bf16)
        prior[b] = before
        mixing = jnp.where(lower, mm(lq[r], lk[r], NT), 0.0).astype(bf16)
        out = mm(mixing, att[r]) + mm(lq[r], before)
        lin[r] = out
        if b < 3:
            run = run + mm(lk[r], att[r], TN)
        scaled = cot[r].astype(f32) * gain[...]
        sums[b : b + 1] = as_row(jnp.sum(out * out, axis=1, keepdims=True))
        sums[4 + b : 5 + b] = as_row(jnp.sum(out * scaled, axis=1, keepdims=True))


def norm_terms(sums, features):
    inv = lax.rsqrt(sums[0:4] / features + eps_norm)
    return inv, inv * inv * inv * sums[4:8] / features


def split_row(row):
    high = row.astype(bf16)
    return high, (row - high.astype(f32)).astype(bf16)


def norm_kernel(features, lq, lin, gain, cot, s0, s1, s2, s3, glin, inv_out, send, local):
    inv, pull = norm_terms(s0[...] + s1[...] + s2[...] + s3[...], features)
    inv_out[0:4] = inv
    inv_out[4:8] = inv
    ggain = jnp.zeros((1, BLK), f32)
    for b in range(4):
        r = slice(b * BLK, (b + 1) * BLK)
        c = cot[r].astype(f32)
        out = lin[r]
        invc = as_cols(inv[b : b + 1])
        ggain = ggain + jnp.sum(c * (out * invc), axis=0, keepdims=True)
        glin[r] = (invc * (c * gain[...]) - out * as_cols(pull[b : b + 1])).astype(bf16)
    run = jnp.zeros((BLK, BLK), f32)
    for b in range(3, -1, -1):
        r = slice(b * BLK, (b + 1) * BLK)
        local[b] = run
        run = run + mm(lq[r], glin[r], TN)
    send[0:BLK] = run.astype(bf16)
    high, rest = split_row(ggain)
    send[BLK : BLK + 8] = jnp.broadcast_to(high, (8, BLK))
    send[BLK + 8 :] = jnp.broadcast_to(rest, (8, BLK))


def sent_kernel(x0, x1, x2, x3, out):
    total = x0[...].astype(f32)
    for r in (x1, x2, x3):
        total = total + r[...].astype(f32)
    high, rest = split_row(total[BLK : BLK + 8] + total[BLK + 8 :])
    state = total[0:BLK].astype(bf16)
    for i in range(NZ):
        out[i, 0:BLK] = state
        out[i, BLK : BLK + 8] = high
        out[i, BLK + 8 :] = rest


def side_kernel(inv, lin, gain, att, glin, lk, lq, prior, mixed, dlq, pairs_t, mix_t):
    lower = lower_mask()
    upper = lax.broadcasted_iota(jnp.int32, (BLK, BLK), 0) <= lax.broadcasted_iota(
        jnp.int32, (BLK, BLK), 1
    )
    for b in range(4):
        r = slice(b * BLK, (b + 1) * BLK)
        normed = lin[r] * as_cols(inv[b : b + 1])
        mixed[r] = (att[r].astype(f32) + gain[...] * normed).astype(bf16)
        pairs = jnp.where(lower, mm(glin[r], att[r], NT), 0.0).astype(bf16)
        dlq[r] = (mm(pairs, lk[r]) + mm(glin[r], prior[b], NT)).astype(bf16)
        pairs_t[b] = jnp.where(upper, mm(att[r], glin[r], NT), 0.0).astype(bf16)
        mix_t[b] = jnp.where(upper, mm(lk[r], lq[r], NT), 0.0).astype(bf16)


def backward_kernel(pos, names, q, lse, att, cot, lq, lk, glin, pairs_t, mix_t, local,
                    x0, x1, x2, x3, zs, pool,
                    dlk, dq, o0, o1, o2, o3, olow, own, back, ggain,
                    acc, gatt, delta, near, lows, sems):
    nsel = names.shape[0]
    scale = BLK ** (-0.5)
    later = jnp.zeros((BLK, BLK), f32)
    for j, r in enumerate((x1, x2, x3)):
        later = later + jnp.where(pos[1] + j + 1 < NX, r[0:BLK].astype(f32), 0.0)
    gg = jnp.zeros((8, BLK), f32)
    for i in range(NZ):
        later = later + jnp.where(pos[0] < i, zs[i, 0:BLK].astype(f32), 0.0)
        gg = gg + zs[i, BLK : BLK + 8].astype(f32) + zs[i, BLK + 8 :].astype(f32)
    ggain[...] = gg
    for b in range(4):
        r = slice(b * BLK, (b + 1) * BLK)
        after = (later + local[b]).astype(bf16)
        dlk[r] = (mm(pairs_t[b], lq[r]) + mm(att[r], after, NT)).astype(bf16)
        g = cot[r].astype(f32) + mm(mix_t[b], glin[r]) + mm(lk[r], after)
        g = g.astype(bf16)
        gatt[r] = g
        delta[b : b + 1] = as_row(
            jnp.sum(g.astype(f32) * att[r].astype(f32), axis=1, keepdims=True)
        )
    acc[...] = jnp.zeros(acc.shape, f32)

    def block(b, carry):
        qb = q[rows(b), :]
        gb = gatt[rows(b), :]
        lse_b = lse[pl.ds(b, 1), :]
        delta_b = delta[pl.ds(b, 1), :]
        dqb = jnp.zeros((BLK, BLK), f32)
        zero = jnp.zeros((BLK, BLK), bf16)
        both = jnp.concatenate(
            [jnp.concatenate([qb, zero], axis=1), jnp.concatenate([zero, gb], axis=1)], axis=0
        )
        for g in range(0, nsel, BGROUP):
            spots = [place_of(pos, names, b, j) for j in range(g, g + BGROUP)]
            keyval = jnp.concatenate([pool[p] for p, _ in spots], axis=0)
            sdp = mm(keyval, both, NT)
            pieces = []
            for i, (_, live) in enumerate(spots):
                r = slice(i * BLK, (i + 1) * BLK)
                piece = sdp[r, 0:BLK] * scale + (jnp.where(live, 0.0, masked_value) - lse_b)
                if g + i == 0:
                    keep = lax.broadcasted_iota(jnp.int32, (BLK, BLK), 0) <= lax.broadcasted_iota(
                        jnp.int32, (BLK, BLK), 1
                    )
                    piece = jnp.where(keep, piece, masked_value)
                pieces.append(jnp.exp(piece))
            p = jnp.concatenate(pieces, axis=0)
            ds = (p * (sdp[:, BLK:] - delta_b)).astype(bf16)
            grads = mm(jnp.concatenate([ds, p.astype(bf16)], axis=1), both)
            dqb = dqb + mm(ds, keyval[:, 0:BLK], TN)
            for i, (spot, _) in enumerate(spots):
                acc[spot] += grads[i * BLK : (i + 1) * BLK]
        dq[rows(b), :] = (dqb * scale).astype(bf16)
        return carry

    lax.fori_loop(0, 4, block, 0)
    for j in range(NX):
        lows[:, j] = acc[NZ * j : NZ * (j + 1), HALF:, BLK:].astype(bf16)
    near[:, 0:BLK] = (acc[0:NZ, :, 0:BLK] * scale).astype(bf16)
    near[:, BLK:] = acc[0:NZ, 0:HALF, BLK:].astype(bf16)
    copies = [pltpu.make_async_copy(lows, olow, sems.at[0]), pltpu.make_async_copy(near, o0, sems.at[1])]
    for c in copies:
        c.start()
    for j, o in ((1, o1), (2, o2), (3, o3)):
        o[:, 0:BLK] = (acc[NZ * j : NZ * (j + 1), :, 0:BLK] * scale).astype(bf16)
        o[:, BLK:] = acc[NZ * j : NZ * (j + 1), 0:HALF, BLK:].astype(bf16)
    own[:, :, 0:BLK] = acc[OWN : OWN + 4, :, 0:BLK] * scale
    own[:, :, BLK:] = acc[OWN : OWN + 4, :, BLK:]
    back[:, 0:BLK] = (acc[PREV, :, 0:BLK] * scale).astype(bf16)
    back[:, BLK:] = acc[PREV, :, BLK:].astype(bf16)
    for c in copies:
        c.wait()


def fold_kernel(a0, a1, a2, a3, low, top, l0, l1, l2, l3):
    total = a0[...].astype(f32) + a1[...].astype(f32) + a2[...].astype(f32) + a3[...].astype(f32)
    top[...] = total.astype(bf16)
    for j, o in enumerate((l0, l1, l2, l3)):
        part = low[0, j].astype(f32)
        for i in range(1, NZ):
            part = part + low[i, j].astype(f32)
        o[...] = part.astype(bf16)


def round_kernel(own, gk, gv):
    for b in range(4):
        r = slice(b * BLK, (b + 1) * BLK)
        gk[r] = own[b, :, 0:BLK].astype(bf16)
        gv[r] = own[b, :, BLK:].astype(bf16)


def finish_kernel(pos, names, own, back, top, l0, l1, l2, l3, gk_in, gv_in, gk, gv):
    mine = chosen_block(pos, names)
    total = top[0].astype(f32)
    for i in range(1, NZ):
        total = total + top[i].astype(f32)
    part = l0[...].astype(f32) + l1[...].astype(f32) + l2[...].astype(f32) + l3[...].astype(f32)
    far_key, far_value = total[0:BLK], jnp.concatenate([total[BLK:], part], axis=0)
    gk[...] = gk_in[...]
    gv[...] = gv_in[...]
    last = mine == 3
    dk = own[3, :, 0:BLK] + back[:, 0:BLK].astype(f32)
    dv = own[3, :, BLK:] + back[:, BLK:].astype(f32)
    gk[rows(3), :] = (dk + jnp.where(last, far_key, 0.0)).astype(bf16)
    gv[rows(3), :] = (dv + jnp.where(last, far_value, 0.0)).astype(bf16)

    @pl.when(mine < 3)
    def _():
        gk[rows(mine), :] = (own[mine, :, 0:BLK] + far_key).astype(bf16)
        gv[rows(mine), :] = (own[mine, :, BLK:] + far_value).astype(bf16)


def turn(value, axis, size, by):
    return lax.ppermute(value, axis, [(i, (i + by) % size) for i in range(size)])


def in_hbm(value):
    return pltpu.with_memory_space_constraint(value, pltpu.HBM)


def swap(value):
    return lax.all_to_all(value, "z", 0, 0, tiled=True)


def turns(values, sign):
    out = []
    for j, value in enumerate(values):
        out.append(turn(value, "x", NX, sign * (j + 1)))
    return out


def per_device(query, key, value, lin_query, lin_key, gain, cotangent, key_block):
    q, k, v, lq, lk, cot = (a[0] for a in (query, key, value, lin_query, lin_key, cotangent))
    width = q.shape[1]
    seq = ("z", "x")
    zi = lax.axis_index("z")
    xi = lax.axis_index("x")
    pos = jnp.stack([zi, xi]).astype(jnp.int32)
    features = float(NY * NC * width)
    key_block = key_block.T
    names = lax.dynamic_slice_in_dim(key_block, (zi * NX + xi) * 4, 4, 1)
    k4 = k.reshape(4, BLK, width)
    v4 = v.reshape(4, BLK, width)
    tile = (BLK, BLK)

    tops, low, last = call(
        pick_kernel,
        [((NZ, TOP, width), bf16), ((HALF, width), bf16), ((BLK, 2 * BLK), bf16)],
        (pos, key_block, in_hbm(k4), in_hbm(v4)),
        [SM, VM, HB, HB],
        [pltpu.VMEM((TOP, width), bf16), pltpu.SemaphoreType.DMA((NZ,))],
        [HB, VM, VM],
    )
    prev = lax.ppermute(last, seq, [(i, i + 1) for i in range(NZ * NX - 1)])
    lows = [low] + [turn(low, "x", NX, j) for j in range(1, NX)]
    (lows,) = call(
        spread_kernel,
        [((NZ, NX, HALF, width), bf16)],
        lows,
        [VM] * 4,
        [pltpu.VMEM((NX, HALF, width), bf16), pltpu.SemaphoreType.DMA((NZ,))],
        [HB],
    )
    tops = swap(tops)
    tops, lows = lax.optimization_barrier((tops, lows))
    far = [tops] + turns([tops] * 3, 1)
    lows = swap(lows)

    att, lse, state, pool = call(
        attend_kernel,
        [((512, width), bf16), ((8, BLK), f32), (tile, bf16), ((POOL, BLK, 2 * BLK), bf16)],
        (pos, names, q, lk, *far, lows, k4, v4, prev),
        [SM, SM, VM, VM] + [AN] * 8,
        [pltpu.VMEM((BLK, names.shape[0] * BLK), f32), pltpu.SemaphoreType.DMA((3 * NX + 3,))],
        vmem=16,
    )

    xs = [state] + [turn(state, "x", NX, j) for j in range(1, NX)]
    (wide,) = call(row_kernel, [((NZ, BLK, width), bf16)], xs, [VM] * 4)
    lin, prior, sums = call(
        linear_kernel,
        [((512, width), f32), ((4, BLK, width), bf16), ((8, BLK), f32)],
        (pos, lq, lk, att, gain, cot, *xs, swap(wide)),
        [SM] + [VM] * 10,
    )
    sums = sums + turn(sums, "c", NC, 1)
    ys = [sums] + [turn(sums, "y", NY, i) for i in range(1, NY)]
    glin, inv, send, local = call(
        functools.partial(norm_kernel, features),
        [((512, width), bf16), ((8, BLK), f32), ((SENT, BLK), bf16), ((4, BLK, BLK), f32)],
        (lq, lin, gain, cot, *ys),
        [VM] * 8,
    )
    ex = [send] + [turn(send, "x", NX, -j) for j in range(1, NX)]
    mixed, dlq, pairs_t, mix_t = call(
        side_kernel,
        [((512, width), bf16), ((512, width), bf16), ((4, BLK, BLK), bf16), ((4, BLK, BLK), bf16)],
        (inv, lin, gain, att, glin, lk, lq, prior),
        [VM] * 8,
    )
    *ex, mixed, dlq, pairs_t, mix_t = lax.optimization_barrier((*ex, mixed, dlq, pairs_t, mix_t))
    (wide,) = call(sent_kernel, [((NZ, SENT, width), bf16)], ex, [VM] * 4)
    outs = call(
        backward_kernel,
        [((512, width), bf16), ((512, width), bf16)]
        + [((NZ, TOP, width), bf16)] * 4
        + [((NZ, NX, HALF, width), bf16), ((4, BLK, 2 * BLK), f32)]
        + [((BLK, 2 * BLK), bf16), ((8, BLK), f32)],
        (pos, names, q, lse, att, cot, lq, lk, glin, pairs_t, mix_t, local, *ex, swap(wide), pool),
        [SM, SM] + [VM] * 16,
        [
            pltpu.VMEM((POOL, BLK, 2 * BLK), f32),
            pltpu.VMEM((512, width), bf16),
            pltpu.VMEM((8, BLK), f32),
            pltpu.VMEM((NZ, TOP, width), bf16),
            pltpu.VMEM((NZ, NX, HALF, width), bf16),
            pltpu.SemaphoreType.DMA((2,)),
        ],
        [VM, VM, HB, VM, VM, VM, HB, VM, VM, VM],
        vmem=24,
    )
    dlk, dq = outs[0], outs[1]
    far_out, low_out, own, back, gg = outs[2:6], outs[6], outs[7], outs[8], outs[9]
    back = lax.ppermute(back, seq, [(i + 1, i) for i in range(NZ * NX - 1)])
    got = [far_out[0]] + turns(far_out[1:], -1)
    folded = call(
        fold_kernel,
        [((NZ, TOP, width), bf16)] + [((HALF, width), bf16)] * NX,
        (*got, swap(low_out)),
        [VM] * 5,
    )
    ends = [folded[1]] + turns(folded[2:], -1)
    gk, gv = call(round_kernel, [((512, width), bf16)] * 2, (own,), [VM])
    gk, gv = call(
        finish_kernel,
        [((512, width), bf16), ((512, width), bf16)],
        (pos, key_block, own, back, swap(folded[0]), *ends, gk, gv),
        [SM] + [VM] * 10,
    )
    lead = lambda a: a[None]
    return (lead(mixed), lead(dq), lead(gk), lead(gv), lead(dlq), lead(dlk), gg[0:1])


def solution(mesh):
    grid = Mesh(mesh.devices.reshape(NZ, NX, NY, NC), ("z", "x", "y", "c"))
    cut = P(("y", "c"), ("z", "x"), None)
    flat = P(("y", "c"), None)
    return jax.shard_map(
        per_device,
        mesh=grid,
        in_specs=(cut, cut, cut, cut, cut, flat, cut, P()),
        out_specs=(cut, cut, cut, cut, cut, cut, flat),
        check_vma=False,
    )
```

```python
import functools

import jax
import jax.numpy as jnp
from jax import lax
from jax.experimental import pallas as pl
from jax.experimental.pallas import tpu as pltpu
from jax.sharding import Mesh, PartitionSpec as P


BLK = 128
NZ, NX, NY, NC = 8, 4, 4, 2
masked_value = -1e30
eps_norm = 1e-05
f32 = jnp.float32
bf16 = jnp.bfloat16
NT = (((1,), (1,)), ((), ()))
TN = (((0,), (0,)), ((), ()))
VM = pl.BlockSpec(memory_space=pltpu.VMEM)
SM = pl.BlockSpec(memory_space=pltpu.SMEM)
AN = pl.BlockSpec(memory_space=pl.ANY)
HB = pl.BlockSpec(memory_space=pltpu.HBM)
FAR = NZ * NX
OWN = FAR
PREV = FAR + 4
HALF = 64
TOP = 192
SENT = 144
POOL = FAR + 5


def mm(a, b, dims=None):
    if dims is None:
        return jnp.dot(a, b, preferred_element_type=f32)
    return lax.dot_general(a, b, dims, preferred_element_type=f32)


def call(body, outs, ins, specs, scratch=(), out_specs=None, vmem=8):
    return pl.pallas_call(
        body,
        out_shape=[jax.ShapeDtypeStruct(s, d) for s, d in outs],
        in_specs=list(specs),
        out_specs=out_specs or [VM] * len(outs),
        scratch_shapes=list(scratch),
        compiler_params=pltpu.CompilerParams(vmem_limit_bytes=vmem << 20),
    )(*ins)


def rows(b):
    return pl.ds(b * BLK, BLK)


def as_row(col):
    return jnp.broadcast_to(col, (BLK, BLK)).T[0:1]


def as_cols(row):
    return jnp.broadcast_to(row, (BLK, BLK)).T


def lower_mask():
    return lax.broadcasted_iota(jnp.int32, (BLK, BLK), 0) >= lax.broadcasted_iota(
        jnp.int32, (BLK, BLK), 1
    )


def chosen_block(pos, names):
    base = pos[0] * 16 + pos[1] * 4
    far = names[...]
    col = lax.broadcasted_iota(jnp.int32, far.shape, 0)
    hit = (col >= 2) & (far >= base) & (far < base + 4)
    return jnp.max(jnp.where(hit, far - base, 0).astype(f32)).astype(jnp.int32)


def pick_kernel(pos, names, k, v, top, low, last, table, keys, values, sems):
    run_copies([(names, table), (k, keys), (v, values)], sems)
    mine = chosen_block(pos, table)
    pairs = []
    for i in range(NZ):
        pairs.append((keys.at[mine], top.at[i, pl.ds(0, BLK)]))
        pairs.append((values.at[mine, pl.ds(0, HALF)], top.at[i, pl.ds(BLK, HALF)]))
    copies = [pltpu.make_async_copy(a, b, sems.at[i]) for i, (a, b) in enumerate(pairs)]
    for c in copies:
        c.start()
    low[...] = values[mine, HALF:, :]
    last[:, 0:BLK] = keys[3]
    last[:, BLK:] = values[3]
    for c in copies:
        c.wait()


def place_of(pos, names, b, j):
    name = names[j, b]
    base = pos[0] * 16 + pos[1] * 4
    live = name >= 0
    if j == 0:
        return OWN + b, live
    if j == 1:
        place = jnp.where(name >= base, OWN + name - base, PREV)
        return jnp.where(live, place, OWN), live
    back_x = jnp.bitwise_and(pos[1] - jnp.bitwise_and(jnp.right_shift(name, 2), 3), NX - 1)
    return jnp.where(live, back_x * NZ + jnp.right_shift(name, 4), OWN), live


def run_copies(pairs, sems):
    copies = [pltpu.make_async_copy(a, b, sems.at[i]) for i, (a, b) in enumerate(pairs)]
    for c in copies:
        c.start()
    for c in copies:
        c.wait()


def pool_pairs(far, low, k, v, prev, pool):
    left, right = pl.ds(0, BLK), pl.ds(BLK, BLK)
    pairs = [(prev, pool.at[PREV])]
    pairs.append((k, pool.at[pl.ds(OWN, 4), :, left]))
    pairs.append((v, pool.at[pl.ds(OWN, 4), :, right]))
    for j, f in enumerate(far):
        spot = pl.ds(NZ * j, NZ)
        pairs.append((f.at[:, pl.ds(0, BLK)], pool.at[spot, :, left]))
        pairs.append((f.at[:, pl.ds(BLK, HALF)], pool.at[spot, pl.ds(0, HALF), right]))
        pairs.append((low.at[:, j], pool.at[spot, pl.ds(HALF, HALF), right]))
    return pairs


GROUP = 4
BGROUP = 20


def attend_kernel(pos, names, q, lk, f0, f1, f2, f3, low, k, v, prev, att, lse, state, pool, s_scr, sems):
    run_copies(pool_pairs((f0, f1, f2, f3), low, k, v, prev, pool), sems)
    nsel = names.shape[0]
    scale = BLK ** (-0.5)

    def block(b, carry):
        qb = q[rows(b), :]
        top = None
        for g in range(0, nsel, GROUP):
            spots = [place_of(pos, names, b, j) for j in range(g, g + GROUP)]
            keys = jnp.concatenate([pool[p, :, 0:BLK] for p, _ in spots], axis=0)
            s = mm(qb, keys, NT)
            for i, (_, live) in enumerate(spots):
                j = g + i
                piece = s[:, i * BLK : (i + 1) * BLK] * scale + jnp.where(live, 0.0, masked_value)
                if j == 0:
                    piece = jnp.where(lower_mask(), piece, masked_value)
                s_scr[:, j * BLK : (j + 1) * BLK] = piece
                top = piece if top is None else jnp.maximum(top, piece)
        row_max = jnp.max(top, axis=1, keepdims=True)
        part = jnp.zeros((BLK, BLK), f32)
        acc = jnp.zeros((BLK, BLK), f32)
        for g in range(0, nsel, GROUP):
            w = jnp.exp(s_scr[:, g * BLK : (g + GROUP) * BLK] - row_max)
            for i in range(GROUP):
                part = part + w[:, i * BLK : (i + 1) * BLK]
            vals = jnp.concatenate(
                [pool[place_of(pos, names, b, j)[0], :, BLK:] for j in range(g, g + GROUP)], axis=0
            )
            acc = acc + mm(w.astype(bf16), vals)
        total = jnp.sum(part, axis=1, keepdims=True)
        att[rows(b), :] = (acc / total).astype(bf16)
        lse[pl.ds(b, 1), :] = as_row(row_max + jnp.log(total))
        return carry

    lax.fori_loop(0, 4, block, 0)
    state[...] = mm(lk[...], att[...], TN).astype(bf16)


def row_kernel(x0, x1, x2, x3, out):
    total = x0[...].astype(f32)
    for r in (x1, x2, x3):
        total = total + r[...].astype(f32)
    total = total.astype(bf16)
    for i in range(NZ):
        out[i] = total


def spread_kernel(l0, l1, l2, l3, out, block, sems):
    for j, r in enumerate((l0, l1, l2, l3)):
        block[j] = r[...]
    run_copies([(block, out.at[i]) for i in range(NZ)], sems)


def within_kernel(lq, lk, att, inner, local):
    lower = lower_mask()
    run = jnp.zeros((BLK, BLK), f32)
    for b in range(4):
        r = slice(b * BLK, (b + 1) * BLK)
        local[b] = run
        mixing = jnp.where(lower, mm(lq[r], lk[r], NT), 0.0).astype(bf16)
        inner[r] = mm(mixing, att[r])
        if b < 3:
            run = run + mm(lk[r], att[r], TN)


def linear_kernel(pos, lq, inner, local, gain, cot, x0, x1, x2, x3, zs, lin, prior, sums):
    run = jnp.zeros((BLK, BLK), f32)
    for j, r in enumerate((x1, x2, x3)):
        run = run + jnp.where(pos[1] > j, r[...].astype(f32), 0.0)
    for i in range(NZ - 1):
        run = run + jnp.where(pos[0] > i, zs[i].astype(f32), 0.0)
    sums[...] = jnp.zeros((8, BLK), f32)
    for b in range(4):
        r = slice(b * BLK, (b + 1) * BLK)
        before = (run + local[b]).astype(bf16)
        prior[b] = before
        out = inner[r] + mm(lq[r], before)
        lin[r] = out
        scaled = cot[r].astype(f32) * gain[...]
        sums[b : b + 1] = as_row(jnp.sum(out * out, axis=1, keepdims=True))
        sums[4 + b : 5 + b] = as_row(jnp.sum(out * scaled, axis=1, keepdims=True))


def norm_terms(sums, features):
    inv = lax.rsqrt(sums[0:4] / features + eps_norm)
    return inv, inv * inv * inv * sums[4:8] / features


def split_row(row):
    high = row.astype(bf16)
    return high, (row - high.astype(f32)).astype(bf16)


def norm_kernel(features, lq, lin, gain, cot, s0, s1, s2, s3, glin, inv_out, send, local):
    inv, pull = norm_terms(s0[...] + s1[...] + s2[...] + s3[...], features)
    inv_out[0:4] = inv
    inv_out[4:8] = inv
    ggain = jnp.zeros((1, BLK), f32)
    for b in range(4):
        r = slice(b * BLK, (b + 1) * BLK)
        c = cot[r].astype(f32)
        out = lin[r]
        invc = as_cols(inv[b : b + 1])
        ggain = ggain + jnp.sum(c * (out * invc), axis=0, keepdims=True)
        glin[r] = (invc * (c * gain[...]) - out * as_cols(pull[b : b + 1])).astype(bf16)
    run = jnp.zeros((BLK, BLK), f32)
    for b in range(3, -1, -1):
        r = slice(b * BLK, (b + 1) * BLK)
        local[b] = run
        run = run + mm(lq[r], glin[r], TN)
    send[0:BLK] = run.astype(bf16)
    high, rest = split_row(ggain)
    send[BLK : BLK + 8] = jnp.broadcast_to(high, (8, BLK))
    send[BLK + 8 :] = jnp.broadcast_to(rest, (8, BLK))


def sent_kernel(x0, x1, x2, x3, out):
    total = x0[...].astype(f32)
    for r in (x1, x2, x3):
        total = total + r[...].astype(f32)
    high, rest = split_row(total[BLK : BLK + 8] + total[BLK + 8 :])
    state = total[0:BLK].astype(bf16)
    for i in range(NZ):
        out[i, 0:BLK] = state
        out[i, BLK : BLK + 8] = high
        out[i, BLK + 8 :] = rest


def side_kernel(inv, lin, gain, att, glin, lk, lq, prior, cot, mixed, dlq, dlk_in, gatt_in):
    lower = lower_mask()
    upper = lax.broadcasted_iota(jnp.int32, (BLK, BLK), 0) <= lax.broadcasted_iota(
        jnp.int32, (BLK, BLK), 1
    )
    for b in range(4):
        r = slice(b * BLK, (b + 1) * BLK)
        normed = lin[r] * as_cols(inv[b : b + 1])
        mixed[r] = (att[r].astype(f32) + gain[...] * normed).astype(bf16)
        pairs = jnp.where(lower, mm(glin[r], att[r], NT), 0.0).astype(bf16)
        dlq[r] = (mm(pairs, lk[r]) + mm(glin[r], prior[b], NT)).astype(bf16)
        pairs_t = jnp.where(upper, mm(att[r], glin[r], NT), 0.0).astype(bf16)
        mix_t = jnp.where(upper, mm(lk[r], lq[r], NT), 0.0).astype(bf16)
        dlk_in[r] = mm(pairs_t, lq[r])
        gatt_in[r] = cot[r].astype(f32) + mm(mix_t, glin[r])


def backward_kernel(pos, names, q, lse, att, lk, dlk_in, gatt_in, local,
                    x0, x1, x2, x3, zs, pool,
                    dlk, dq, o0, o1, o2, o3, olow, own, back, ggain,
                    acc, gatt, delta, near, lows, sems):
    nsel = names.shape[0]
    scale = BLK ** (-0.5)
    later = jnp.zeros((BLK, BLK), f32)
    for j, r in enumerate((x1, x2, x3)):
        later = later + jnp.where(pos[1] + j + 1 < NX, r[0:BLK].astype(f32), 0.0)
    gg = jnp.zeros((8, BLK), f32)
    for i in range(NZ):
        later = later + jnp.where(pos[0] < i, zs[i, 0:BLK].astype(f32), 0.0)
        gg = gg + zs[i, BLK : BLK + 8].astype(f32) + zs[i, BLK + 8 :].astype(f32)
    ggain[...] = gg
    for b in range(4):
        r = slice(b * BLK, (b + 1) * BLK)
        after = (later + local[b]).astype(bf16)
        dlk[r] = (dlk_in[r] + mm(att[r], after, NT)).astype(bf16)
        g = (gatt_in[r] + mm(lk[r], after)).astype(bf16)
        gatt[r] = g
        delta[b : b + 1] = as_row(
            jnp.sum(g.astype(f32) * att[r].astype(f32), axis=1, keepdims=True)
        )
    acc[...] = jnp.zeros(acc.shape, f32)

    def block(b, carry):
        qb = q[rows(b), :]
        gb = gatt[rows(b), :]
        lse_b = lse[pl.ds(b, 1), :]
        delta_b = delta[pl.ds(b, 1), :]
        dqb = jnp.zeros((BLK, BLK), f32)
        zero = jnp.zeros((BLK, BLK), bf16)
        both = jnp.concatenate(
            [jnp.concatenate([qb, zero], axis=1), jnp.concatenate([zero, gb], axis=1)], axis=0
        )
        for g in range(0, nsel, BGROUP):
            spots = [place_of(pos, names, b, j) for j in range(g, g + BGROUP)]
            keyval = jnp.concatenate([pool[p] for p, _ in spots], axis=0)
            sdp = mm(keyval, both, NT)
            pieces = []
            for i, (_, live) in enumerate(spots):
                r = slice(i * BLK, (i + 1) * BLK)
                piece = sdp[r, 0:BLK] * scale + (jnp.where(live, 0.0, masked_value) - lse_b)
                if g + i == 0:
                    keep = lax.broadcasted_iota(jnp.int32, (BLK, BLK), 0) <= lax.broadcasted_iota(
                        jnp.int32, (BLK, BLK), 1
                    )
                    piece = jnp.where(keep, piece, masked_value)
                pieces.append(jnp.exp(piece))
            p = jnp.concatenate(pieces, axis=0)
            ds = (p * (sdp[:, BLK:] - delta_b)).astype(bf16)
            grads = mm(jnp.concatenate([ds, p.astype(bf16)], axis=1), both)
            dqb = dqb + mm(ds, keyval[:, 0:BLK], TN)
            for i, (spot, _) in enumerate(spots):
                acc[spot] += grads[i * BLK : (i + 1) * BLK]
        dq[rows(b), :] = (dqb * scale).astype(bf16)
        return carry

    lax.fori_loop(0, 4, block, 0)
    for j in range(NX):
        lows[:, j] = acc[NZ * j : NZ * (j + 1), HALF:, BLK:].astype(bf16)
    near[:, 0:BLK] = (acc[0:NZ, :, 0:BLK] * scale).astype(bf16)
    near[:, BLK:] = acc[0:NZ, 0:HALF, BLK:].astype(bf16)
    copies = [pltpu.make_async_copy(lows, olow, sems.at[0]), pltpu.make_async_copy(near, o0, sems.at[1])]
    for c in copies:
        c.start()
    for j, o in ((1, o1), (2, o2), (3, o3)):
        o[:, 0:BLK] = (acc[NZ * j : NZ * (j + 1), :, 0:BLK] * scale).astype(bf16)
        o[:, BLK:] = acc[NZ * j : NZ * (j + 1), 0:HALF, BLK:].astype(bf16)
    own[:, :, 0:BLK] = acc[OWN : OWN + 4, :, 0:BLK] * scale
    own[:, :, BLK:] = acc[OWN : OWN + 4, :, BLK:]
    back[:, 0:BLK] = (acc[PREV, :, 0:BLK] * scale).astype(bf16)
    back[:, BLK:] = acc[PREV, :, BLK:].astype(bf16)
    for c in copies:
        c.wait()


def fold_kernel(a0, a1, a2, a3, low, top, l0, l1, l2, l3):
    total = a0[...].astype(f32) + a1[...].astype(f32) + a2[...].astype(f32) + a3[...].astype(f32)
    top[...] = total.astype(bf16)
    for j, o in enumerate((l0, l1, l2, l3)):
        part = low[0, j].astype(f32)
        for i in range(1, NZ):
            part = part + low[i, j].astype(f32)
        o[...] = part.astype(bf16)


def round_kernel(pos, names, own, gk, gv, rest):
    mine = chosen_block(pos, names)
    for b in range(4):
        r = slice(b * BLK, (b + 1) * BLK)
        gk[r] = own[b, :, 0:BLK].astype(bf16)
        gv[r] = own[b, :, BLK:].astype(bf16)
    rest[0] = own[mine]
    rest[1] = own[3]


def finish_kernel(pos, names, rest, back, top, l0, l1, l2, l3, gk_in, gv_in, gk, gv):
    mine = chosen_block(pos, names)
    total = top[0].astype(f32)
    for i in range(1, NZ):
        total = total + top[i].astype(f32)
    part = l0[...].astype(f32) + l1[...].astype(f32) + l2[...].astype(f32) + l3[...].astype(f32)
    far_key, far_value = total[0:BLK], jnp.concatenate([total[BLK:], part], axis=0)
    gk[...] = gk_in[...]
    gv[...] = gv_in[...]
    last = mine == 3
    dk = rest[1, :, 0:BLK] + back[:, 0:BLK].astype(f32)
    dv = rest[1, :, BLK:] + back[:, BLK:].astype(f32)
    gk[rows(3), :] = (dk + jnp.where(last, far_key, 0.0)).astype(bf16)
    gv[rows(3), :] = (dv + jnp.where(last, far_value, 0.0)).astype(bf16)

    @pl.when(mine < 3)
    def _():
        gk[rows(mine), :] = (rest[0, :, 0:BLK] + far_key).astype(bf16)
        gv[rows(mine), :] = (rest[0, :, BLK:] + far_value).astype(bf16)


def turn(value, axis, size, by):
    return lax.ppermute(value, axis, [(i, (i + by) % size) for i in range(size)])


def in_hbm(value):
    return pltpu.with_memory_space_constraint(value, pltpu.HBM)


def swap(value):
    return lax.all_to_all(value, "z", 0, 0, tiled=True)


def turns(values, sign):
    out = []
    for j, value in enumerate(values):
        out.append(turn(value, "x", NX, sign * (j + 1)))
    return out


def per_device(query, key, value, lin_query, lin_key, gain, cotangent, key_block):
    q, k, v, lq, lk, cot = (a[0] for a in (query, key, value, lin_query, lin_key, cotangent))
    width = q.shape[1]
    seq = ("z", "x")
    zi = lax.axis_index("z")
    xi = lax.axis_index("x")
    pos = jnp.stack([zi, xi]).astype(jnp.int32)
    features = float(NY * NC * width)
    key_block = key_block.T
    names = lax.dynamic_slice_in_dim(key_block, (zi * NX + xi) * 4, 4, 1)
    k4 = k.reshape(4, BLK, width)
    v4 = v.reshape(4, BLK, width)
    tile = (BLK, BLK)

    tops, low, last = call(
        pick_kernel,
        [((NZ, TOP, width), bf16), ((HALF, width), bf16), ((BLK, 2 * BLK), bf16)],
        (pos, in_hbm(key_block), in_hbm(k4), in_hbm(v4)),
        [SM, HB, HB, HB],
        [
            pltpu.VMEM(key_block.shape, jnp.int32),
            pltpu.VMEM((4, BLK, width), bf16),
            pltpu.VMEM((4, BLK, width), bf16),
            pltpu.SemaphoreType.DMA((2 * NZ,)),
        ],
        [HB, VM, VM],
    )
    prev = lax.ppermute(last, seq, [(i, i + 1) for i in range(NZ * NX - 1)])
    lows = [low] + [turn(low, "x", NX, j) for j in range(1, NX)]
    (lows,) = call(
        spread_kernel,
        [((NZ, NX, HALF, width), bf16)],
        lows,
        [VM] * 4,
        [pltpu.VMEM((NX, HALF, width), bf16), pltpu.SemaphoreType.DMA((NZ,))],
        [HB],
    )
    tops = swap(tops)
    tops, lows = lax.optimization_barrier((tops, lows))
    far = [tops] + turns([tops] * 3, 1)
    lows = swap(lows)

    att, lse, state, pool = call(
        attend_kernel,
        [((512, width), bf16), ((8, BLK), f32), (tile, bf16), ((POOL, BLK, 2 * BLK), bf16)],
        (pos, names, q, lk, *far, lows, k4, v4, prev),
        [SM, SM, VM, VM] + [AN] * 8,
        [pltpu.VMEM((BLK, names.shape[0] * BLK), f32), pltpu.SemaphoreType.DMA((3 * NX + 3,))],
        vmem=16,
    )

    xs = [state] + [turn(state, "x", NX, j) for j in range(1, NX)]
    inner, local = call(
        within_kernel,
        [((512, width), f32), ((4, BLK, width), f32)],
        (lq, lk, att),
        [VM] * 3,
    )
    *xs, inner, local = lax.optimization_barrier((*xs, inner, local))
    (wide,) = call(row_kernel, [((NZ, BLK, width), bf16)], xs, [VM] * 4)
    lin, prior, sums = call(
        linear_kernel,
        [((512, width), f32), ((4, BLK, width), bf16), ((8, BLK), f32)],
        (pos, lq, inner, local, gain, cot, *xs, swap(wide)),
        [SM] + [VM] * 10,
    )
    sums = sums + turn(sums, "c", NC, 1)
    ys = [sums] + [turn(sums, "y", NY, i) for i in range(1, NY)]
    glin, inv, send, local = call(
        functools.partial(norm_kernel, features),
        [((512, width), bf16), ((8, BLK), f32), ((SENT, BLK), bf16), ((4, BLK, BLK), f32)],
        (lq, lin, gain, cot, *ys),
        [VM] * 8,
    )
    ex = [send] + [turn(send, "x", NX, -j) for j in range(1, NX)]
    mixed, dlq, dlk_in, gatt_in = call(
        side_kernel,
        [((512, width), bf16), ((512, width), bf16), ((512, width), f32), ((512, width), f32)],
        (inv, lin, gain, att, glin, lk, lq, prior, cot),
        [VM] * 9,
    )
    *ex, mixed, dlq, dlk_in, gatt_in = lax.optimization_barrier((*ex, mixed, dlq, dlk_in, gatt_in))
    (wide,) = call(sent_kernel, [((NZ, SENT, width), bf16)], ex, [VM] * 4)
    outs = call(
        backward_kernel,
        [((512, width), bf16), ((512, width), bf16)]
        + [((NZ, TOP, width), bf16)] * 4
        + [((NZ, NX, HALF, width), bf16), ((4, BLK, 2 * BLK), f32)]
        + [((BLK, 2 * BLK), bf16), ((8, BLK), f32)],
        (pos, names, q, lse, att, lk, dlk_in, gatt_in, local, *ex, swap(wide), pool),
        [SM, SM] + [VM] * 13,
        [
            pltpu.VMEM((POOL, BLK, 2 * BLK), f32),
            pltpu.VMEM((512, width), bf16),
            pltpu.VMEM((8, BLK), f32),
            pltpu.VMEM((NZ, TOP, width), bf16),
            pltpu.VMEM((NZ, NX, HALF, width), bf16),
            pltpu.SemaphoreType.DMA((2,)),
        ],
        [VM, VM, HB, VM, VM, VM, HB, VM, VM, VM],
        vmem=24,
    )
    dlk, dq = outs[0], outs[1]
    far_out, low_out, own, back, gg = outs[2:6], outs[6], outs[7], outs[8], outs[9]
    back = lax.ppermute(back, seq, [(i + 1, i) for i in range(NZ * NX - 1)])
    got = [far_out[0]] + turns(far_out[1:], -1)
    folded = call(
        fold_kernel,
        [((NZ, TOP, width), bf16)] + [((HALF, width), bf16)] * NX,
        (*got, swap(low_out)),
        [VM] * 5,
    )
    ends = [folded[1]] + turns(folded[2:], -1)
    gk, gv, rest = call(
        round_kernel,
        [((512, width), bf16)] * 2 + [((2, BLK, 2 * BLK), f32)],
        (pos, key_block, own),
        [SM, VM, VM],
    )
    gk, gv = call(
        finish_kernel,
        [((512, width), bf16), ((512, width), bf16)],
        (pos, key_block, rest, back, swap(folded[0]), *ends, gk, gv),
        [SM] + [VM] * 10,
    )
    lead = lambda a: a[None]
    return (lead(mixed), lead(dq), lead(gk), lead(gv), lead(dlq), lead(dlk), gg[0:1])


def solution(mesh):
    grid = Mesh(mesh.devices.reshape(NZ, NX, NY, NC), ("z", "x", "y", "c"))
    cut = P(("y", "c"), ("z", "x"), None)
    flat = P(("y", "c"), None)
    return jax.shard_map(
        per_device,
        mesh=grid,
        in_specs=(cut, cut, cut, cut, cut, flat, cut, P()),
        out_specs=(cut, cut, cut, cut, cut, cut, flat),
        check_vma=False,
    )
```

```python
import functools

import jax
import jax.numpy as jnp
from jax import lax
from jax.experimental import pallas as pl
from jax.experimental.pallas import tpu as pltpu
from jax.sharding import Mesh, PartitionSpec as P


BLK = 128
NZ, NX, NY, NC = 8, 4, 4, 2
masked_value = -1e30
eps_norm = 1e-05
f32 = jnp.float32
bf16 = jnp.bfloat16
NT = (((1,), (1,)), ((), ()))
TN = (((0,), (0,)), ((), ()))
VM = pl.BlockSpec(memory_space=pltpu.VMEM)
SM = pl.BlockSpec(memory_space=pltpu.SMEM)
AN = pl.BlockSpec(memory_space=pl.ANY)
HB = pl.BlockSpec(memory_space=pltpu.HBM)
FAR = NZ * NX
OWN = FAR
PREV = FAR + 4
HALF = 64
TOP = 192
REST = 48
FIRST = 208
MOST = FIRST - BLK
SENT = 144
POOL = FAR + 5


def mm(a, b, dims=None):
    if dims is None:
        return jnp.dot(a, b, preferred_element_type=f32)
    return lax.dot_general(a, b, dims, preferred_element_type=f32)


def call(body, outs, ins, specs, scratch=(), out_specs=None, vmem=8):
    return pl.pallas_call(
        body,
        out_shape=[jax.ShapeDtypeStruct(s, d) for s, d in outs],
        in_specs=list(specs),
        out_specs=out_specs or [VM] * len(outs),
        scratch_shapes=list(scratch),
        compiler_params=pltpu.CompilerParams(vmem_limit_bytes=vmem << 20),
    )(*ins)


def rows(b):
    return pl.ds(b * BLK, BLK)


def as_row(col):
    return jnp.broadcast_to(col, (BLK, BLK)).T[0:1]


def as_cols(row):
    return jnp.broadcast_to(row, (BLK, BLK)).T


def lower_mask():
    return lax.broadcasted_iota(jnp.int32, (BLK, BLK), 0) >= lax.broadcasted_iota(
        jnp.int32, (BLK, BLK), 1
    )


def chosen_block(pos, names):
    base = pos[0] * 16 + pos[1] * 4
    far = names[...]
    col = lax.broadcasted_iota(jnp.int32, far.shape, 0)
    hit = (col >= 2) & (far >= base) & (far < base + 4)
    return jnp.max(jnp.where(hit, far - base, 0).astype(f32)).astype(jnp.int32)


def pick_kernel(pos, names, k, v, top, low, last, table, keys, values, sems):
    run_copies([(names, table), (k, keys), (v, values)], sems)
    mine = chosen_block(pos, table)
    pairs = []
    for i in range(NZ):
        pairs.append((keys.at[mine], top.at[i, pl.ds(0, BLK)]))
        pairs.append((values.at[mine, pl.ds(0, MOST)], top.at[i, pl.ds(BLK, MOST)]))
    copies = [pltpu.make_async_copy(a, b, sems.at[i]) for i, (a, b) in enumerate(pairs)]
    for c in copies:
        c.start()
    low[...] = values[mine, MOST:, :]
    last[:, 0:BLK] = keys[3]
    last[:, BLK:] = values[3]
    for c in copies:
        c.wait()


def place_of(pos, names, b, j):
    name = names[j, b]
    base = pos[0] * 16 + pos[1] * 4
    live = name >= 0
    if j == 0:
        return OWN + b, live
    if j == 1:
        place = jnp.where(name >= base, OWN + name - base, PREV)
        return jnp.where(live, place, OWN), live
    back_x = jnp.bitwise_and(pos[1] - jnp.bitwise_and(jnp.right_shift(name, 2), 3), NX - 1)
    return jnp.where(live, back_x * NZ + jnp.right_shift(name, 4), OWN), live


def run_copies(pairs, sems):
    copies = [pltpu.make_async_copy(a, b, sems.at[i]) for i, (a, b) in enumerate(pairs)]
    for c in copies:
        c.start()
    for c in copies:
        c.wait()


def pool_pairs(far, low, k, v, prev, pool):
    left, right = pl.ds(0, BLK), pl.ds(BLK, BLK)
    pairs = [(prev, pool.at[PREV])]
    pairs.append((k, pool.at[pl.ds(OWN, 4), :, left]))
    pairs.append((v, pool.at[pl.ds(OWN, 4), :, right]))
    for j, f in enumerate(far):
        spot = pl.ds(NZ * j, NZ)
        pairs.append((f.at[:, pl.ds(0, BLK)], pool.at[spot, :, left]))
        pairs.append((f.at[:, pl.ds(BLK, MOST)], pool.at[spot, pl.ds(0, MOST), right]))
        pairs.append((low.at[:, j], pool.at[spot, pl.ds(MOST, REST), right]))
    return pairs


GROUP = 4
BGROUP = 20


def attend_kernel(pos, names, q, lk, f0, f1, f2, f3, low, k, v, prev, att, lse, state, pool, s_scr, sems):
    run_copies(pool_pairs((f0, f1, f2, f3), low, k, v, prev, pool), sems)
    nsel = names.shape[0]
    scale = BLK ** (-0.5)

    def block(b, carry):
        qb = q[rows(b), :]
        top = None
        for g in range(0, nsel, GROUP):
            spots = [place_of(pos, names, b, j) for j in range(g, g + GROUP)]
            keys = jnp.concatenate([pool[p, :, 0:BLK] for p, _ in spots], axis=0)
            s = mm(qb, keys, NT)
            for i, (_, live) in enumerate(spots):
                j = g + i
                piece = s[:, i * BLK : (i + 1) * BLK] * scale + jnp.where(live, 0.0, masked_value)
                if j == 0:
                    piece = jnp.where(lower_mask(), piece, masked_value)
                s_scr[:, j * BLK : (j + 1) * BLK] = piece
                top = piece if top is None else jnp.maximum(top, piece)
        row_max = jnp.max(top, axis=1, keepdims=True)
        part = jnp.zeros((BLK, BLK), f32)
        acc = jnp.zeros((BLK, BLK), f32)
        for g in range(0, nsel, GROUP):
            w = jnp.exp(s_scr[:, g * BLK : (g + GROUP) * BLK] - row_max)
            for i in range(GROUP):
                part = part + w[:, i * BLK : (i + 1) * BLK]
            vals = jnp.concatenate(
                [pool[place_of(pos, names, b, j)[0], :, BLK:] for j in range(g, g + GROUP)], axis=0
            )
            acc = acc + mm(w.astype(bf16), vals)
        total = jnp.sum(part, axis=1, keepdims=True)
        att[rows(b), :] = (acc / total).astype(bf16)
        lse[pl.ds(b, 1), :] = as_row(row_max + jnp.log(total))
        return carry

    lax.fori_loop(0, 4, block, 0)
    state[...] = mm(lk[...], att[...], TN).astype(bf16)


def row_kernel(x0, x1, out):
    total = (x0[...].astype(f32) + x1[...].astype(f32)).astype(bf16)
    for i in range(NZ):
        out[i] = total


def spread_kernel(l0, l1, l2, l3, out, block, sems):
    for j, r in enumerate((l0, l1, l2, l3)):
        block[j] = r[...]
    run_copies([(block, out.at[i]) for i in range(NZ)], sems)


def within_kernel(lq, lk, att, inner, local):
    lower = lower_mask()
    run = jnp.zeros((BLK, BLK), f32)
    for b in range(4):
        r = slice(b * BLK, (b + 1) * BLK)
        local[b] = run
        mixing = jnp.where(lower, mm(lq[r], lk[r], NT), 0.0).astype(bf16)
        inner[r] = mm(mixing, att[r])
        if b < 3:
            run = run + mm(lk[r], att[r], TN)


def linear_kernel(pos, lq, inner, local, gain, cot, near, pair, zs, lin, prior, sums):
    run = jnp.where(jnp.bitwise_and(pos[1], 1) == 1, near[...].astype(f32), 0.0)
    run = run + jnp.where(pos[1] >= 2, pair[...].astype(f32), 0.0)
    for i in range(NZ - 1):
        run = run + jnp.where(pos[0] > i, zs[i].astype(f32), 0.0)
    sums[...] = jnp.zeros((8, BLK), f32)
    for b in range(4):
        r = slice(b * BLK, (b + 1) * BLK)
        before = (run + local[b]).astype(bf16)
        prior[b] = before
        out = inner[r] + mm(lq[r], before)
        lin[r] = out
        scaled = cot[r].astype(f32) * gain[...]
        sums[b : b + 1] = as_row(jnp.sum(out * out, axis=1, keepdims=True))
        sums[4 + b : 5 + b] = as_row(jnp.sum(out * scaled, axis=1, keepdims=True))


def norm_terms(sums, features):
    inv = lax.rsqrt(sums[0:4] / features + eps_norm)
    return inv, inv * inv * inv * sums[4:8] / features


def split_row(row):
    high = row.astype(bf16)
    return high, (row - high.astype(f32)).astype(bf16)


def norm_kernel(features, lq, lin, gain, cot, s0, s1, glin, inv_out, send, local):
    inv, pull = norm_terms(s0[...] + s1[...], features)
    inv_out[0:4] = inv
    inv_out[4:8] = inv
    ggain = jnp.zeros((1, BLK), f32)
    for b in range(4):
        r = slice(b * BLK, (b + 1) * BLK)
        c = cot[r].astype(f32)
        out = lin[r]
        invc = as_cols(inv[b : b + 1])
        ggain = ggain + jnp.sum(c * (out * invc), axis=0, keepdims=True)
        glin[r] = (invc * (c * gain[...]) - out * as_cols(pull[b : b + 1])).astype(bf16)
    run = jnp.zeros((BLK, BLK), f32)
    for b in range(3, -1, -1):
        r = slice(b * BLK, (b + 1) * BLK)
        local[b] = run
        run = run + mm(lq[r], glin[r], TN)
    send[0:BLK] = run.astype(bf16)
    high, rest = split_row(ggain)
    send[BLK : BLK + 8] = jnp.broadcast_to(high, (8, BLK))
    send[BLK + 8 :] = jnp.broadcast_to(rest, (8, BLK))


def joined(a, b):
    total = a[...].astype(f32) + b[...].astype(f32)
    high, rest = split_row(total[BLK : BLK + 8] + total[BLK + 8 :])
    return total[0:BLK].astype(bf16), high, rest


def pair_kernel(x0, x1, out):
    out[0:BLK], out[BLK : BLK + 8], out[BLK + 8 :] = joined(x0, x1)


def sent_kernel(x0, x1, out):
    state, high, rest = joined(x0, x1)
    for i in range(NZ):
        out[i, 0:BLK] = state
        out[i, BLK : BLK + 8] = high
        out[i, BLK + 8 :] = rest


def side_kernel(inv, lin, gain, att, glin, lk, lq, prior, cot, mixed, dlq, dlk_in, gatt_in):
    lower = lower_mask()
    upper = lax.broadcasted_iota(jnp.int32, (BLK, BLK), 0) <= lax.broadcasted_iota(
        jnp.int32, (BLK, BLK), 1
    )
    for b in range(4):
        r = slice(b * BLK, (b + 1) * BLK)
        normed = lin[r] * as_cols(inv[b : b + 1])
        mixed[r] = (att[r].astype(f32) + gain[...] * normed).astype(bf16)
        pairs = jnp.where(lower, mm(glin[r], att[r], NT), 0.0).astype(bf16)
        dlq[r] = (mm(pairs, lk[r]) + mm(glin[r], prior[b], NT)).astype(bf16)
        pairs_t = jnp.where(upper, mm(att[r], glin[r], NT), 0.0).astype(bf16)
        mix_t = jnp.where(upper, mm(lk[r], lq[r], NT), 0.0).astype(bf16)
        dlk_in[r] = mm(pairs_t, lq[r])
        gatt_in[r] = cot[r].astype(f32) + mm(mix_t, glin[r])


def backward_kernel(pos, names, q, lse, att, lk, dlk_in, gatt_in, local,
                    near, pair, zs, pool,
                    dlk, dq, o0, o1, o2, o3, olow, own, back, ggain,
                    acc, gatt, delta, dlk_buf, dq_buf, far_buf, lows, sems):
    nsel = names.shape[0]
    scale = BLK ** (-0.5)
    later = jnp.where(jnp.bitwise_and(pos[1], 1) == 0, near[0:BLK].astype(f32), 0.0)
    later = later + jnp.where(pos[1] < 2, pair[0:BLK].astype(f32), 0.0)
    gg = jnp.zeros((8, BLK), f32)
    for i in range(NZ):
        later = later + jnp.where(pos[0] < i, zs[i, 0:BLK].astype(f32), 0.0)
        gg = gg + zs[i, BLK : BLK + 8].astype(f32) + zs[i, BLK + 8 :].astype(f32)
    ggain[...] = gg
    for b in range(4):
        r = slice(b * BLK, (b + 1) * BLK)
        after = (later + local[b]).astype(bf16)
        dlk_buf[r] = (dlk_in[r] + mm(att[r], after, NT)).astype(bf16)
        g = (gatt_in[r] + mm(lk[r], after)).astype(bf16)
        gatt[r] = g
        delta[b : b + 1] = as_row(
            jnp.sum(g.astype(f32) * att[r].astype(f32), axis=1, keepdims=True)
        )
    copies = [pltpu.make_async_copy(dlk_buf, dlk, sems.at[0])]
    copies[0].start()
    acc[...] = jnp.zeros(acc.shape, f32)

    def block(b, carry):
        qb = q[rows(b), :]
        gb = gatt[rows(b), :]
        lse_b = lse[pl.ds(b, 1), :]
        delta_b = delta[pl.ds(b, 1), :]
        dqb = jnp.zeros((BLK, BLK), f32)
        zero = jnp.zeros((BLK, BLK), bf16)
        both = jnp.concatenate(
            [jnp.concatenate([qb, zero], axis=1), jnp.concatenate([zero, gb], axis=1)], axis=0
        )
        for g in range(0, nsel, BGROUP):
            spots = [place_of(pos, names, b, j) for j in range(g, g + BGROUP)]
            keyval = jnp.concatenate([pool[p] for p, _ in spots], axis=0)
            sdp = mm(keyval, both, NT)
            pieces = []
            for i, (_, live) in enumerate(spots):
                r = slice(i * BLK, (i + 1) * BLK)
                piece = sdp[r, 0:BLK] * scale + (jnp.where(live, 0.0, masked_value) - lse_b)
                if g + i == 0:
                    keep = lax.broadcasted_iota(jnp.int32, (BLK, BLK), 0) <= lax.broadcasted_iota(
                        jnp.int32, (BLK, BLK), 1
                    )
                    piece = jnp.where(keep, piece, masked_value)
                pieces.append(jnp.exp(piece))
            p = jnp.concatenate(pieces, axis=0)
            ds = (p * (sdp[:, BLK:] - delta_b)).astype(bf16)
            grads = mm(jnp.concatenate([ds, p.astype(bf16)], axis=1), both)
            dqb = dqb + mm(ds, keyval[:, 0:BLK], TN)
            for i, (spot, _) in enumerate(spots):
                acc[spot] += grads[i * BLK : (i + 1) * BLK]
        dq_buf[rows(b), :] = (dqb * scale).astype(bf16)
        return carry

    lax.fori_loop(0, 4, block, 0)

    def send(src, dst):
        copies.append(pltpu.make_async_copy(src, dst, sems.at[len(copies)]))
        copies[-1].start()

    send(dq_buf, dq)
    for j, o in ((1, o1), (2, o2), (3, o3), (0, o0)):
        spot = slice(NZ * j, NZ * (j + 1))
        far_buf[j, :, 0:BLK] = (acc[spot, :, 0:BLK] * scale).astype(bf16)
        far_buf[j, :, BLK:] = acc[spot, 0:HALF, BLK:].astype(bf16)
        send(far_buf.at[j], o)
    for j in range(NX):
        lows[:, j] = acc[NZ * j : NZ * (j + 1), HALF:, BLK:].astype(bf16)
    send(lows, olow)
    own[:, :, 0:BLK] = acc[OWN : OWN + 4, :, 0:BLK] * scale
    own[:, :, BLK:] = acc[OWN : OWN + 4, :, BLK:]
    back[:, 0:BLK] = (acc[PREV, :, 0:BLK] * scale).astype(bf16)
    back[:, BLK:] = acc[PREV, :, BLK:].astype(bf16)
    for c in copies:
        c.wait()


def fold_kernel(a0, a1, a2, a3, low, top, l0, l1, l2, l3):
    total = a0[...].astype(f32) + a1[...].astype(f32) + a2[...].astype(f32) + a3[...].astype(f32)
    top[...] = total.astype(bf16)
    for j, o in enumerate((l0, l1, l2, l3)):
        part = low[0, j].astype(f32)
        for i in range(1, NZ):
            part = part + low[i, j].astype(f32)
        o[...] = part.astype(bf16)


def round_kernel(pos, names, own, gk, gv, rest):
    mine = chosen_block(pos, names)
    for b in range(4):
        r = slice(b * BLK, (b + 1) * BLK)
        gk[r] = own[b, :, 0:BLK].astype(bf16)
        gv[r] = own[b, :, BLK:].astype(bf16)
    rest[0] = own[mine]
    rest[1] = own[3]


def finish_kernel(pos, names, rest, back, top, l0, l1, l2, l3, gk_in, gv_in, gk, gv):
    mine = chosen_block(pos, names)
    total = top[0].astype(f32)
    for i in range(1, NZ):
        total = total + top[i].astype(f32)
    part = l0[...].astype(f32) + l1[...].astype(f32) + l2[...].astype(f32) + l3[...].astype(f32)
    far_key, far_value = total[0:BLK], jnp.concatenate([total[BLK:], part], axis=0)
    gk[...] = gk_in[...]
    gv[...] = gv_in[...]
    last = mine == 3
    dk = rest[1, :, 0:BLK] + back[:, 0:BLK].astype(f32)
    dv = rest[1, :, BLK:] + back[:, BLK:].astype(f32)
    gk[rows(3), :] = (dk + jnp.where(last, far_key, 0.0)).astype(bf16)
    gv[rows(3), :] = (dv + jnp.where(last, far_value, 0.0)).astype(bf16)

    @pl.when(mine < 3)
    def _():
        gk[rows(mine), :] = (rest[0, :, 0:BLK] + far_key).astype(bf16)
        gv[rows(mine), :] = (rest[0, :, BLK:] + far_value).astype(bf16)


def turn(value, axis, size, by):
    return lax.ppermute(value, axis, [(i, (i + by) % size) for i in range(size)])


def flip(value, axis, size, bit):
    return lax.ppermute(value, axis, [(i, i ^ bit) for i in range(size)])


def in_hbm(value):
    return pltpu.with_memory_space_constraint(value, pltpu.HBM)


def swap(value):
    return lax.all_to_all(value, "z", 0, 0, tiled=True)


def turns(values, sign):
    out = []
    for j, value in enumerate(values):
        out.append(turn(value, "x", NX, sign * (j + 1)))
    return out


def per_device(query, key, value, lin_query, lin_key, gain, cotangent, key_block):
    q, k, v, lq, lk, cot = (a[0] for a in (query, key, value, lin_query, lin_key, cotangent))
    width = q.shape[1]
    seq = ("z", "x")
    zi = lax.axis_index("z")
    xi = lax.axis_index("x")
    pos = jnp.stack([zi, xi]).astype(jnp.int32)
    features = float(NY * NC * width)
    key_block = key_block.T
    names = lax.dynamic_slice_in_dim(key_block, (zi * NX + xi) * 4, 4, 1)
    k4 = k.reshape(4, BLK, width)
    v4 = v.reshape(4, BLK, width)
    tile = (BLK, BLK)

    tops, low, last = call(
        pick_kernel,
        [((NZ, FIRST, width), bf16), ((REST, width), bf16), ((BLK, 2 * BLK), bf16)],
        (pos, in_hbm(key_block), in_hbm(k4), in_hbm(v4)),
        [SM, HB, HB, HB],
        [
            pltpu.VMEM(key_block.shape, jnp.int32),
            pltpu.VMEM((4, BLK, width), bf16),
            pltpu.VMEM((4, BLK, width), bf16),
            pltpu.SemaphoreType.DMA((2 * NZ,)),
        ],
        [HB, VM, VM],
    )
    prev = lax.ppermute(last, seq, [(i, i + 1) for i in range(NZ * NX - 1)])
    lows = [low] + [turn(low, "x", NX, j) for j in range(1, NX)]
    (lows,) = call(
        spread_kernel,
        [((NZ, NX, REST, width), bf16)],
        lows,
        [VM] * 4,
        [pltpu.VMEM((NX, REST, width), bf16), pltpu.SemaphoreType.DMA((NZ,))],
        [HB],
    )
    tops = swap(tops)
    tops, lows = lax.optimization_barrier((tops, lows))
    far = [tops] + turns([tops] * 3, 1)
    lows = swap(lows)

    att, lse, state, pool = call(
        attend_kernel,
        [((512, width), bf16), ((8, BLK), f32), (tile, bf16), ((POOL, BLK, 2 * BLK), bf16)],
        (pos, names, q, lk, *far, lows, k4, v4, prev),
        [SM, SM, VM, VM] + [AN] * 8,
        [pltpu.VMEM((BLK, names.shape[0] * BLK), f32), pltpu.SemaphoreType.DMA((3 * NX + 3,))],
        vmem=16,
    )

    near = flip(state, "x", NX, 1)
    half = (state.astype(f32) + near.astype(f32)).astype(bf16)
    pair = flip(half, "x", NX, 2)
    inner, local = call(
        within_kernel,
        [((512, width), f32), ((4, BLK, width), f32)],
        (lq, lk, att),
        [VM] * 3,
    )
    pair, inner, local = lax.optimization_barrier((pair, inner, local))
    (wide,) = call(row_kernel, [((NZ, BLK, width), bf16)], (half, pair), [VM] * 2)
    lin, prior, sums = call(
        linear_kernel,
        [((512, width), f32), ((4, BLK, width), bf16), ((8, BLK), f32)],
        (pos, lq, inner, local, gain, cot, near, pair, swap(wide)),
        [SM] + [VM] * 8,
    )
    sums = sums + flip(sums, "c", NC, 1)
    sums = sums + flip(sums, "y", NY, 1)
    others = flip(sums, "y", NY, 2)
    glin, inv, send, local = call(
        functools.partial(norm_kernel, features),
        [((512, width), bf16), ((8, BLK), f32), ((SENT, BLK), bf16), ((4, BLK, BLK), f32)],
        (lq, lin, gain, cot, sums, others),
        [VM] * 6,
    )
    near = flip(send, "x", NX, 1)
    (half,) = call(pair_kernel, [((SENT, width), bf16)], (send, near), [VM] * 2)
    pair = flip(half, "x", NX, 2)
    mixed, dlq, dlk_in, gatt_in = call(
        side_kernel,
        [((512, width), bf16), ((512, width), bf16), ((512, width), f32), ((512, width), f32)],
        (inv, lin, gain, att, glin, lk, lq, prior, cot),
        [VM] * 9,
    )
    pair, mixed, dlq, dlk_in, gatt_in = lax.optimization_barrier(
        (pair, mixed, dlq, dlk_in, gatt_in)
    )
    (wide,) = call(sent_kernel, [((NZ, SENT, width), bf16)], (half, pair), [VM] * 2)
    outs = call(
        backward_kernel,
        [((512, width), bf16), ((512, width), bf16)]
        + [((NZ, TOP, width), bf16)] * 4
        + [((NZ, NX, HALF, width), bf16), ((4, BLK, 2 * BLK), f32)]
        + [((BLK, 2 * BLK), bf16), ((8, BLK), f32)],
        (pos, names, q, lse, att, lk, dlk_in, gatt_in, local, near, pair, swap(wide), pool),
        [SM, SM] + [VM] * 11,
        [
            pltpu.VMEM((POOL, BLK, 2 * BLK), f32),
            pltpu.VMEM((512, width), bf16),
            pltpu.VMEM((8, BLK), f32),
            pltpu.VMEM((512, width), bf16),
            pltpu.VMEM((512, width), bf16),
            pltpu.VMEM((NX, NZ, TOP, width), bf16),
            pltpu.VMEM((NZ, NX, HALF, width), bf16),
            pltpu.SemaphoreType.DMA((NX + 3,)),
        ],
        [HB] * 7 + [VM, VM, VM],
        vmem=24,
    )
    dlk, dq = outs[0], outs[1]
    far_out, low_out, own, back, gg = outs[2:6], outs[6], outs[7], outs[8], outs[9]
    back = lax.ppermute(back, seq, [(i + 1, i) for i in range(NZ * NX - 1)])
    got = [far_out[0]] + turns(far_out[1:], -1)
    folded = call(
        fold_kernel,
        [((NZ, TOP, width), bf16)] + [((HALF, width), bf16)] * NX,
        (*got, swap(low_out)),
        [VM] * 5,
    )
    ends = [folded[1]] + turns(folded[2:], -1)
    gk, gv, rest = call(
        round_kernel,
        [((512, width), bf16)] * 2 + [((2, BLK, 2 * BLK), f32)],
        (pos, key_block, own),
        [SM, VM, VM],
    )
    gk, gv = call(
        finish_kernel,
        [((512, width), bf16), ((512, width), bf16)],
        (pos, key_block, rest, back, swap(folded[0]), *ends, gk, gv),
        [SM] + [VM] * 10,
    )
    lead = lambda a: a[None]
    return (lead(mixed), lead(dq), lead(gk), lead(gv), lead(dlq), lead(dlk), gg[0:1])


def solution(mesh):
    grid = Mesh(mesh.devices.reshape(NZ, NX, NY, NC), ("z", "x", "y", "c"))
    cut = P(("y", "c"), ("z", "x"), None)
    flat = P(("y", "c"), None)
    return jax.shard_map(
        per_device,
        mesh=grid,
        in_specs=(cut, cut, cut, cut, cut, flat, cut, P()),
        out_specs=(cut, cut, cut, cut, cut, cut, flat),
        check_vma=False,
    )
```

```python
import functools

import jax
import jax.numpy as jnp
from jax import lax
from jax.experimental import pallas as pl
from jax.experimental.pallas import tpu as pltpu
from jax.sharding import Mesh, PartitionSpec as P


BLK = 128
NZ, NX, NY, NC = 8, 4, 4, 2
masked_value = -1e30
eps_norm = 1e-05
f32 = jnp.float32
bf16 = jnp.bfloat16
NT = (((1,), (1,)), ((), ()))
TN = (((0,), (0,)), ((), ()))
VM = pl.BlockSpec(memory_space=pltpu.VMEM)
SM = pl.BlockSpec(memory_space=pltpu.SMEM)
AN = pl.BlockSpec(memory_space=pl.ANY)
HB = pl.BlockSpec(memory_space=pltpu.HBM)
FAR = NZ * NX
OWN = FAR
PREV = FAR + 4
HALF = 64
TOP = 192
REST = 48
FIRST = 208
MOST = FIRST - BLK
SENT = 144
POOL = FAR + 5


def mm(a, b, dims=None):
    if dims is None:
        return jnp.dot(a, b, preferred_element_type=f32)
    return lax.dot_general(a, b, dims, preferred_element_type=f32)


def call(body, outs, ins, specs, scratch=(), out_specs=None, vmem=8):
    return pl.pallas_call(
        body,
        out_shape=[jax.ShapeDtypeStruct(s, d) for s, d in outs],
        in_specs=list(specs),
        out_specs=out_specs or [VM] * len(outs),
        scratch_shapes=list(scratch),
        compiler_params=pltpu.CompilerParams(vmem_limit_bytes=vmem << 20),
    )(*ins)


def rows(b):
    return pl.ds(b * BLK, BLK)


def as_row(col):
    return jnp.broadcast_to(col, (BLK, BLK)).T[0:1]


def as_cols(row):
    return jnp.broadcast_to(row, (BLK, BLK)).T


def lower_mask():
    return lax.broadcasted_iota(jnp.int32, (BLK, BLK), 0) >= lax.broadcasted_iota(
        jnp.int32, (BLK, BLK), 1
    )


def chosen_block(pos, names):
    base = pos[0] * 16 + pos[1] * 4
    far = names[...]
    col = lax.broadcasted_iota(jnp.int32, far.shape, 0)
    hit = (col >= 2) & (far >= base) & (far < base + 4)
    return jnp.max(jnp.where(hit, far - base, 0).astype(f32)).astype(jnp.int32)


def pick_kernel(pos, names, k, v, top, low, last, table, keys, values, sems):
    run_copies([(names, table), (k, keys), (v, values)], sems)
    mine = chosen_block(pos, table)
    pairs = []
    for i in range(NZ):
        pairs.append((keys.at[mine], top.at[i, pl.ds(0, BLK)]))
        pairs.append((values.at[mine, pl.ds(0, MOST)], top.at[i, pl.ds(BLK, MOST)]))
    copies = [pltpu.make_async_copy(a, b, sems.at[i]) for i, (a, b) in enumerate(pairs)]
    for c in copies:
        c.start()
    low[...] = values[mine, MOST:, :]
    last[:, 0:BLK] = keys[3]
    last[:, BLK:] = values[3]
    for c in copies:
        c.wait()


def place_of(pos, names, b, j):
    name = names[j, b]
    base = pos[0] * 16 + pos[1] * 4
    live = name >= 0
    if j == 0:
        return OWN + b, live
    if j == 1:
        place = jnp.where(name >= base, OWN + name - base, PREV)
        return jnp.where(live, place, OWN), live
    back_x = jnp.bitwise_and(pos[1] - jnp.bitwise_and(jnp.right_shift(name, 2), 3), NX - 1)
    return jnp.where(live, back_x * NZ + jnp.right_shift(name, 4), OWN), live


def run_copies(pairs, sems):
    copies = [pltpu.make_async_copy(a, b, sems.at[i]) for i, (a, b) in enumerate(pairs)]
    for c in copies:
        c.start()
    for c in copies:
        c.wait()


def pool_pairs(far, low, k, v, prev, pool):
    left, right = pl.ds(0, BLK), pl.ds(BLK, BLK)
    pairs = [(prev, pool.at[PREV])]
    pairs.append((k, pool.at[pl.ds(OWN, 4), :, left]))
    pairs.append((v, pool.at[pl.ds(OWN, 4), :, right]))
    for j, f in enumerate(far):
        spot = pl.ds(NZ * j, NZ)
        pairs.append((f.at[:, pl.ds(0, BLK)], pool.at[spot, :, left]))
        pairs.append((f.at[:, pl.ds(BLK, MOST)], pool.at[spot, pl.ds(0, MOST), right]))
        pairs.append((low.at[:, j], pool.at[spot, pl.ds(MOST, REST), right]))
    return pairs


GROUP = 4
BGROUP = 20


def attend_kernel(pos, names, q, lk, f0, f1, f2, f3, low, k, v, prev, att, lse, state, pool, s_scr, sems):
    run_copies(pool_pairs((f0, f1, f2, f3), low, k, v, prev, pool), sems)
    nsel = names.shape[0]
    scale = BLK ** (-0.5)

    def block(b, carry):
        qb = q[rows(b), :]
        top = None
        for g in range(0, nsel, GROUP):
            spots = [place_of(pos, names, b, j) for j in range(g, g + GROUP)]
            keys = jnp.concatenate([pool[p, :, 0:BLK] for p, _ in spots], axis=0)
            s = mm(qb, keys, NT)
            for i, (_, live) in enumerate(spots):
                j = g + i
                piece = s[:, i * BLK : (i + 1) * BLK] * scale + jnp.where(live, 0.0, masked_value)
                if j == 0:
                    piece = jnp.where(lower_mask(), piece, masked_value)
                s_scr[:, j * BLK : (j + 1) * BLK] = piece
                top = piece if top is None else jnp.maximum(top, piece)
        row_max = jnp.max(top, axis=1, keepdims=True)
        part = jnp.zeros((BLK, BLK), f32)
        acc = jnp.zeros((BLK, BLK), f32)
        for g in range(0, nsel, GROUP):
            w = jnp.exp(s_scr[:, g * BLK : (g + GROUP) * BLK] - row_max)
            for i in range(GROUP):
                part = part + w[:, i * BLK : (i + 1) * BLK]
            vals = jnp.concatenate(
                [pool[place_of(pos, names, b, j)[0], :, BLK:] for j in range(g, g + GROUP)], axis=0
            )
            acc = acc + mm(w.astype(bf16), vals)
        total = jnp.sum(part, axis=1, keepdims=True)
        att[rows(b), :] = (acc / total).astype(bf16)
        lse[pl.ds(b, 1), :] = as_row(row_max + jnp.log(total))
        return carry

    lax.fori_loop(0, 4, block, 0, unroll=4)
    state[...] = mm(lk[...], att[...], TN).astype(bf16)


def row_kernel(x0, x1, x2, x3, out):
    total = x0[...].astype(f32)
    for r in (x1, x2, x3):
        total = total + r[...].astype(f32)
    total = total.astype(bf16)
    for i in range(NZ):
        out[i] = total


def spread_kernel(l0, l1, l2, l3, out, block, sems):
    for j, r in enumerate((l0, l1, l2, l3)):
        block[j] = r[...]
    run_copies([(block, out.at[i]) for i in range(NZ)], sems)


def within_kernel(lq, lk, att, inner, local):
    lower = lower_mask()
    run = jnp.zeros((BLK, BLK), f32)
    for b in range(4):
        r = slice(b * BLK, (b + 1) * BLK)
        local[b] = run
        mixing = jnp.where(lower, mm(lq[r], lk[r], NT), 0.0).astype(bf16)
        inner[r] = mm(mixing, att[r])
        if b < 3:
            run = run + mm(lk[r], att[r], TN)


def linear_kernel(pos, lq, inner, local, gain, cot, x0, x1, x2, x3, zs, lin, prior, sums):
    run = jnp.zeros((BLK, BLK), f32)
    for j, r in enumerate((x1, x2, x3)):
        run = run + jnp.where(pos[1] > j, r[...].astype(f32), 0.0)
    for i in range(NZ - 1):
        run = run + jnp.where(pos[0] > i, zs[i].astype(f32), 0.0)
    sums[...] = jnp.zeros((8, BLK), f32)
    for b in range(4):
        r = slice(b * BLK, (b + 1) * BLK)
        before = (run + local[b]).astype(bf16)
        prior[b] = before
        out = inner[r] + mm(lq[r], before)
        lin[r] = out
        scaled = cot[r].astype(f32) * gain[...]
        sums[b : b + 1] = as_row(jnp.sum(out * out, axis=1, keepdims=True))
        sums[4 + b : 5 + b] = as_row(jnp.sum(out * scaled, axis=1, keepdims=True))


def norm_terms(sums, features):
    inv = lax.rsqrt(sums[0:4] / features + eps_norm)
    return inv, inv * inv * inv * sums[4:8] / features


def split_row(row):
    high = row.astype(bf16)
    return high, (row - high.astype(f32)).astype(bf16)


def norm_kernel(features, lq, lin, gain, cot, s0, s1, s2, s3, glin, inv_out, send, local):
    inv, pull = norm_terms(s0[...] + s1[...] + s2[...] + s3[...], features)
    inv_out[0:4] = inv
    inv_out[4:8] = inv
    ggain = jnp.zeros((1, BLK), f32)
    for b in range(4):
        r = slice(b * BLK, (b + 1) * BLK)
        c = cot[r].astype(f32)
        out = lin[r]
        invc = as_cols(inv[b : b + 1])
        ggain = ggain + jnp.sum(c * (out * invc), axis=0, keepdims=True)
        glin[r] = (invc * (c * gain[...]) - out * as_cols(pull[b : b + 1])).astype(bf16)
    run = jnp.zeros((BLK, BLK), f32)
    for b in range(3, -1, -1):
        r = slice(b * BLK, (b + 1) * BLK)
        local[b] = run
        run = run + mm(lq[r], glin[r], TN)
    send[0:BLK] = run.astype(bf16)
    high, rest = split_row(ggain)
    send[BLK : BLK + 8] = jnp.broadcast_to(high, (8, BLK))
    send[BLK + 8 :] = jnp.broadcast_to(rest, (8, BLK))


def sent_kernel(x0, x1, x2, x3, out):
    total = x0[...].astype(f32)
    for r in (x1, x2, x3):
        total = total + r[...].astype(f32)
    high, rest = split_row(total[BLK : BLK + 8] + total[BLK + 8 :])
    state = total[0:BLK].astype(bf16)
    for i in range(NZ):
        out[i, 0:BLK] = state
        out[i, BLK : BLK + 8] = high
        out[i, BLK + 8 :] = rest


def side_kernel(inv, lin, gain, att, glin, lk, lq, prior, cot, mixed, dlq, dlk_in, gatt_in):
    lower = lower_mask()
    upper = lax.broadcasted_iota(jnp.int32, (BLK, BLK), 0) <= lax.broadcasted_iota(
        jnp.int32, (BLK, BLK), 1
    )
    for b in range(4):
        r = slice(b * BLK, (b + 1) * BLK)
        normed = lin[r] * as_cols(inv[b : b + 1])
        mixed[r] = (att[r].astype(f32) + gain[...] * normed).astype(bf16)
        pairs = jnp.where(lower, mm(glin[r], att[r], NT), 0.0).astype(bf16)
        dlq[r] = (mm(pairs, lk[r]) + mm(glin[r], prior[b], NT)).astype(bf16)
        pairs_t = jnp.where(upper, mm(att[r], glin[r], NT), 0.0).astype(bf16)
        mix_t = jnp.where(upper, mm(lk[r], lq[r], NT), 0.0).astype(bf16)
        dlk_in[r] = mm(pairs_t, lq[r])
        gatt_in[r] = cot[r].astype(f32) + mm(mix_t, glin[r])


def backward_kernel(pos, names, q, lse, att, lk, dlk_in, gatt_in, local,
                    x0, x1, x2, x3, zs, pool,
                    dlk, dq, o0, o1, o2, o3, olow, own, back, ggain,
                    acc, gatt, delta, dlk_buf, dq_buf, far_buf, lows, sems):
    nsel = names.shape[0]
    scale = BLK ** (-0.5)
    later = jnp.zeros((BLK, BLK), f32)
    for j, r in enumerate((x1, x2, x3)):
        later = later + jnp.where(pos[1] + j + 1 < NX, r[0:BLK].astype(f32), 0.0)
    gg = jnp.zeros((8, BLK), f32)
    for i in range(NZ):
        later = later + jnp.where(pos[0] < i, zs[i, 0:BLK].astype(f32), 0.0)
        gg = gg + zs[i, BLK : BLK + 8].astype(f32) + zs[i, BLK + 8 :].astype(f32)
    ggain[...] = gg
    for b in range(4):
        r = slice(b * BLK, (b + 1) * BLK)
        after = (later + local[b]).astype(bf16)
        dlk_buf[r] = (dlk_in[r] + mm(att[r], after, NT)).astype(bf16)
        g = (gatt_in[r] + mm(lk[r], after)).astype(bf16)
        gatt[r] = g
        delta[b : b + 1] = as_row(
            jnp.sum(g.astype(f32) * att[r].astype(f32), axis=1, keepdims=True)
        )
    copies = [pltpu.make_async_copy(dlk_buf, dlk, sems.at[0])]
    copies[0].start()
    acc[...] = jnp.zeros(acc.shape, f32)

    def block(b, carry):
        qb = q[rows(b), :]
        gb = gatt[rows(b), :]
        lse_b = lse[pl.ds(b, 1), :]
        delta_b = delta[pl.ds(b, 1), :]
        dqb = jnp.zeros((BLK, BLK), f32)
        zero = jnp.zeros((BLK, BLK), bf16)
        both = jnp.concatenate(
            [jnp.concatenate([qb, zero], axis=1), jnp.concatenate([zero, gb], axis=1)], axis=0
        )
        for g in range(0, nsel, BGROUP):
            spots = [place_of(pos, names, b, j) for j in range(g, g + BGROUP)]
            keyval = jnp.concatenate([pool[p] for p, _ in spots], axis=0)
            sdp = mm(keyval, both, NT)
            pieces = []
            for i, (_, live) in enumerate(spots):
                r = slice(i * BLK, (i + 1) * BLK)
                piece = sdp[r, 0:BLK] * scale + (jnp.where(live, 0.0, masked_value) - lse_b)
                if g + i == 0:
                    keep = lax.broadcasted_iota(jnp.int32, (BLK, BLK), 0) <= lax.broadcasted_iota(
                        jnp.int32, (BLK, BLK), 1
                    )
                    piece = jnp.where(keep, piece, masked_value)
                pieces.append(jnp.exp(piece))
            p = jnp.concatenate(pieces, axis=0)
            ds = (p * (sdp[:, BLK:] - delta_b)).astype(bf16)
            grads = mm(jnp.concatenate([ds, p.astype(bf16)], axis=1), both)
            dqb = dqb + mm(ds, keyval[:, 0:BLK], TN)
            for i, (spot, _) in enumerate(spots):
                acc[spot] += grads[i * BLK : (i + 1) * BLK]
        dq_buf[rows(b), :] = (dqb * scale).astype(bf16)
        return carry

    lax.fori_loop(0, 4, block, 0, unroll=4)

    def send(src, dst):
        copies.append(pltpu.make_async_copy(src, dst, sems.at[len(copies)]))
        copies[-1].start()

    send(dq_buf, dq)
    for j, o in ((1, o1), (2, o2), (3, o3), (0, o0)):
        spot = slice(NZ * j, NZ * (j + 1))
        far_buf[j, :, 0:BLK] = (acc[spot, :, 0:BLK] * scale).astype(bf16)
        far_buf[j, :, BLK:] = acc[spot, 0:HALF, BLK:].astype(bf16)
        send(far_buf.at[j], o)
    for j in range(NX):
        lows[:, j] = acc[NZ * j : NZ * (j + 1), HALF:, BLK:].astype(bf16)
    send(lows, olow)
    own[:, :, 0:BLK] = acc[OWN : OWN + 4, :, 0:BLK] * scale
    own[:, :, BLK:] = acc[OWN : OWN + 4, :, BLK:]
    back[:, 0:BLK] = (acc[PREV, :, 0:BLK] * scale).astype(bf16)
    back[:, BLK:] = acc[PREV, :, BLK:].astype(bf16)
    for c in copies:
        c.wait()


def fold_kernel(a0, a1, a2, a3, low, top, l0, l1, l2, l3):
    total = a0[...].astype(f32) + a1[...].astype(f32) + a2[...].astype(f32) + a3[...].astype(f32)
    top[...] = total.astype(bf16)
    for j, o in enumerate((l0, l1, l2, l3)):
        part = low[0, j].astype(f32)
        for i in range(1, NZ):
            part = part + low[i, j].astype(f32)
        o[...] = part.astype(bf16)


def round_kernel(pos, names, own, gk, gv, rest):
    mine = chosen_block(pos, names)
    for b in range(4):
        r = slice(b * BLK, (b + 1) * BLK)
        gk[r] = own[b, :, 0:BLK].astype(bf16)
        gv[r] = own[b, :, BLK:].astype(bf16)
    rest[0] = own[mine]
    rest[1] = own[3]


def finish_kernel(pos, names, rest, back, top, l0, l1, l2, l3, gk_in, gv_in, gk, gv):
    mine = chosen_block(pos, names)
    total = top[0].astype(f32)
    for i in range(1, NZ):
        total = total + top[i].astype(f32)
    part = l0[...].astype(f32) + l1[...].astype(f32) + l2[...].astype(f32) + l3[...].astype(f32)
    far_key, far_value = total[0:BLK], jnp.concatenate([total[BLK:], part], axis=0)
    gk[...] = gk_in[...]
    gv[...] = gv_in[...]
    last = mine == 3
    dk = rest[1, :, 0:BLK] + back[:, 0:BLK].astype(f32)
    dv = rest[1, :, BLK:] + back[:, BLK:].astype(f32)
    gk[rows(3), :] = (dk + jnp.where(last, far_key, 0.0)).astype(bf16)
    gv[rows(3), :] = (dv + jnp.where(last, far_value, 0.0)).astype(bf16)

    @pl.when(mine < 3)
    def _():
        gk[rows(mine), :] = (rest[0, :, 0:BLK] + far_key).astype(bf16)
        gv[rows(mine), :] = (rest[0, :, BLK:] + far_value).astype(bf16)


def turn(value, axis, size, by):
    return lax.ppermute(value, axis, [(i, (i + by) % size) for i in range(size)])


def in_hbm(value):
    return pltpu.with_memory_space_constraint(value, pltpu.HBM)


def swap(value):
    return lax.all_to_all(value, "z", 0, 0, tiled=True)


def turns(values, sign):
    out = []
    for j, value in enumerate(values):
        out.append(turn(value, "x", NX, sign * (j + 1)))
    return out


def per_device(query, key, value, lin_query, lin_key, gain, cotangent, key_block):
    q, k, v, lq, lk, cot = (a[0] for a in (query, key, value, lin_query, lin_key, cotangent))
    width = q.shape[1]
    seq = ("z", "x")
    zi = lax.axis_index("z")
    xi = lax.axis_index("x")
    pos = jnp.stack([zi, xi]).astype(jnp.int32)
    features = float(NY * NC * width)
    key_block = key_block.T
    names = lax.dynamic_slice_in_dim(key_block, (zi * NX + xi) * 4, 4, 1)
    k4 = k.reshape(4, BLK, width)
    v4 = v.reshape(4, BLK, width)
    tile = (BLK, BLK)

    tops, low, last = call(
        pick_kernel,
        [((NZ, FIRST, width), bf16), ((REST, width), bf16), ((BLK, 2 * BLK), bf16)],
        (pos, in_hbm(key_block), in_hbm(k4), in_hbm(v4)),
        [SM, HB, HB, HB],
        [
            pltpu.VMEM(key_block.shape, jnp.int32),
            pltpu.VMEM((4, BLK, width), bf16),
            pltpu.VMEM((4, BLK, width), bf16),
            pltpu.SemaphoreType.DMA((2 * NZ,)),
        ],
        [HB, VM, VM],
    )
    prev = lax.ppermute(last, seq, [(i, i + 1) for i in range(NZ * NX - 1)])
    lows = [low] + [turn(low, "x", NX, j) for j in range(1, NX)]
    (lows,) = call(
        spread_kernel,
        [((NZ, NX, REST, width), bf16)],
        lows,
        [VM] * 4,
        [pltpu.VMEM((NX, REST, width), bf16), pltpu.SemaphoreType.DMA((NZ,))],
        [HB],
    )
    tops = swap(tops)
    tops, lows = lax.optimization_barrier((tops, lows))
    far = [tops] + turns([tops] * 3, 1)
    lows = swap(lows)

    att, lse, state, pool = call(
        attend_kernel,
        [((512, width), bf16), ((8, BLK), f32), (tile, bf16), ((POOL, BLK, 2 * BLK), bf16)],
        (pos, names, q, lk, *far, lows, k4, v4, prev),
        [SM, SM, VM, VM] + [AN] * 8,
        [pltpu.VMEM((BLK, names.shape[0] * BLK), f32), pltpu.SemaphoreType.DMA((3 * NX + 3,))],
        vmem=16,
    )

    xs = [state] + [turn(state, "x", NX, j) for j in range(1, NX)]
    inner, local = call(
        within_kernel,
        [((512, width), f32), ((4, BLK, width), f32)],
        (lq, lk, att),
        [VM] * 3,
    )
    *xs, inner, local = lax.optimization_barrier((*xs, inner, local))
    (wide,) = call(row_kernel, [((NZ, BLK, width), bf16)], xs, [VM] * 4)
    lin, prior, sums = call(
        linear_kernel,
        [((512, width), f32), ((4, BLK, width), bf16), ((8, BLK), f32)],
        (pos, lq, inner, local, gain, cot, *xs, swap(wide)),
        [SM] + [VM] * 10,
    )
    sums = sums + turn(sums, "c", NC, 1)
    ys = [sums] + [turn(sums, "y", NY, i) for i in range(1, NY)]
    glin, inv, send, local = call(
        functools.partial(norm_kernel, features),
        [((512, width), bf16), ((8, BLK), f32), ((SENT, BLK), bf16), ((4, BLK, BLK), f32)],
        (lq, lin, gain, cot, *ys),
        [VM] * 8,
    )
    ex = [send] + [turn(send, "x", NX, -j) for j in range(1, NX)]
    mixed, dlq, dlk_in, gatt_in = call(
        side_kernel,
        [((512, width), bf16), ((512, width), bf16), ((512, width), f32), ((512, width), f32)],
        (inv, lin, gain, att, glin, lk, lq, prior, cot),
        [VM] * 9,
    )
    *ex, mixed, dlq, dlk_in, gatt_in = lax.optimization_barrier((*ex, mixed, dlq, dlk_in, gatt_in))
    (wide,) = call(sent_kernel, [((NZ, SENT, width), bf16)], ex, [VM] * 4)
    outs = call(
        backward_kernel,
        [((512, width), bf16), ((512, width), bf16)]
        + [((NZ, TOP, width), bf16)] * 4
        + [((NZ, NX, HALF, width), bf16), ((4, BLK, 2 * BLK), f32)]
        + [((BLK, 2 * BLK), bf16), ((8, BLK), f32)],
        (pos, names, q, lse, att, lk, dlk_in, gatt_in, local, *ex, swap(wide), pool),
        [SM, SM] + [VM] * 13,
        [
            pltpu.VMEM((POOL, BLK, 2 * BLK), f32),
            pltpu.VMEM((512, width), bf16),
            pltpu.VMEM((8, BLK), f32),
            pltpu.VMEM((512, width), bf16),
            pltpu.VMEM((512, width), bf16),
            pltpu.VMEM((NX, NZ, TOP, width), bf16),
            pltpu.VMEM((NZ, NX, HALF, width), bf16),
            pltpu.SemaphoreType.DMA((NX + 3,)),
        ],
        [HB] * 7 + [VM, VM, VM],
        vmem=24,
    )
    dlk, dq = outs[0], outs[1]
    far_out, low_out, own, back, gg = outs[2:6], outs[6], outs[7], outs[8], outs[9]
    back = lax.ppermute(back, seq, [(i + 1, i) for i in range(NZ * NX - 1)])
    got = [far_out[0]] + turns(far_out[1:], -1)
    folded = call(
        fold_kernel,
        [((NZ, TOP, width), bf16)] + [((HALF, width), bf16)] * NX,
        (*got, swap(low_out)),
        [VM] * 5,
    )
    ends = [folded[1]] + turns(folded[2:], -1)
    gk, gv, rest = call(
        round_kernel,
        [((512, width), bf16)] * 2 + [((2, BLK, 2 * BLK), f32)],
        (pos, key_block, own),
        [SM, VM, VM],
    )
    gk, gv = call(
        finish_kernel,
        [((512, width), bf16), ((512, width), bf16)],
        (pos, key_block, rest, back, swap(folded[0]), *ends, gk, gv),
        [SM] + [VM] * 10,
    )
    lead = lambda a: a[None]
    return (lead(mixed), lead(dq), lead(gk), lead(gv), lead(dlq), lead(dlk), gg[0:1])


def solution(mesh):
    grid = Mesh(mesh.devices.reshape(NZ, NX, NY, NC), ("z", "x", "y", "c"))
    cut = P(("y", "c"), ("z", "x"), None)
    flat = P(("y", "c"), None)
    return jax.shard_map(
        per_device,
        mesh=grid,
        in_specs=(cut, cut, cut, cut, cut, flat, cut, P()),
        out_specs=(cut, cut, cut, cut, cut, cut, flat),
        check_vma=False,
    )
```
